256 devices in a mesh: px: 8 (over y, core), py: 32 (over x, z).
Axes of the slice: x: 4, y: 4, z: 8, core: 2. Of those that a mesh axis runs over, the one named last changes fastest.
Arguments:
- source: float32 [256, 512, 256], P('px', 'py'), may hold values from -3.5 to 3.7
- density: float32 [256, 512, 256], P('px', 'py'), may hold values from 0.25 to 4
Outputs:
- pressure: float32 [256, 512, 256], P('px', 'py')
The draws below stay inside these ranges and needn't reach their ends.
All inputs are finite; a program needn't handle non-finite values.
Results may differ from the reference program's by a relative error of at most 0.0001.
Values sent between devices are 32-bit elements; how exact they have to be, the bound alone decides.
No kernel may reach another device: no remote copies, remote signals or barrier semaphores. Data moves between devices by JAX's collectives and lax.ppermute only.
A program may use at most 128 MiB of HBM per device.

```python
import math
import jax
import jax.numpy as jnp
from jax import lax

LEVELS = 4
COARSE = 8
NX = 256
NY = 512
NZ = 256


def draw_source(key, part):
    subkeys = jax.random.split(jax.random.fold_in(key, 11), 3)
    periods = jax.random.uniform(subkeys[0], (3,), jnp.float32, 40.0, 72.0)
    phases = jax.random.uniform(subkeys[1], (3,), jnp.float32, 0.0, 2.0 * math.pi)
    row_pos = jnp.arange(NX, dtype=jnp.float32)[:, None, None]
    col_pos = jnp.arange(NY, dtype=jnp.float32)[None, :, None]
    plane_pos = jnp.arange(NZ, dtype=jnp.float32)[None, None, :]
    waves = jnp.sin(2.0 * math.pi * row_pos / periods[0] + phases[0]) + jnp.sin(2.0 * math.pi * col_pos / periods[1] + phases[1]) + jnp.sin(2.0 * math.pi * plane_pos / periods[2] + phases[2])
    rough_part = jnp.clip(jax.random.normal(subkeys[2], (NX, NY, NZ), jnp.float32), -3.5, 3.5)
    smooth_part = 0.08 * (1.0 + 0.3 * waves)
    return (rough_part + smooth_part).astype(jnp.float32)


def block_scale(own_key, shape, pieces, low, top_value):
    def one(position, blocks):
        steps = jax.random.uniform(jax.random.fold_in(jax.random.fold_in(own_key, 6), position), (blocks,), jnp.float32, low / len(pieces), top_value / len(pieces))
        return jnp.repeat(jnp.exp(steps), shape[position] // blocks).reshape((-1,) + (1,) * (len(shape) - position - 1))

    loudness = one(*pieces[0])
    for cut in pieces[1:]:
        loudness = loudness * one(*cut)
    return loudness


def setup_inputs(seed: int = 0) -> dict:
    key_of = jax.random.split(jax.random.key(seed), 3)
    return {
        "source": draw_source(jax.random.fold_in(key_of[2], 71), 0),
        "density": jnp.clip(jnp.exp(math.log(4.0) - 2.7725887 * jax.random.uniform(key_of[1], (NX, NY, NZ), jnp.float32) ** block_scale(key_of[1], (NX, NY, NZ), ((0, 8), (1, 32)), -0.2, 0.2)), 0.25, 4.0),
    }


RELAXATION = 0.8


def operate(field_pad, mobility_pad, factor):
    full_pad = jnp.pad(field_pad, ((0, 0), (0, 0), (1, 1)))
    along_x = full_pad[:, 1:-1, 1:-1]
    mob_x = mobility_pad[:, 1:-1, 1:-1]
    flux_x = 0.5 * (mob_x[:-1] + mob_x[1:]) * (along_x[:-1] - along_x[1:])
    summed = flux_x[1:] - flux_x[:-1]
    along_y = full_pad[1:-1, :, 1:-1]
    mob_y = mobility_pad[1:-1, :, 1:-1]
    flux_y = 0.5 * (mob_y[:, :-1] + mob_y[:, 1:]) * (along_y[:, :-1] - along_y[:, 1:])
    summed = summed + (flux_y[:, 1:] - flux_y[:, :-1])
    along_z = full_pad[1:-1, 1:-1, :]
    mob_z = mobility_pad[1:-1, 1:-1, :]
    flux_z = 0.5 * (mob_z[:, :, :-1] + mob_z[:, :, 1:]) * (along_z[:, :, :-1] - along_z[:, :, 1:])
    summed = summed + (flux_z[:, :, 1:] - flux_z[:, :, :-1])
    return factor * summed


def diagonal(mobility_pad, factor):
    centre_mobility = mobility_pad[1:-1, 1:-1, 1:-1]
    summed = 3.0 * centre_mobility
    summed = summed + 0.5 * (mobility_pad[:-2, 1:-1, 1:-1] + mobility_pad[2:, 1:-1, 1:-1])
    summed = summed + 0.5 * (mobility_pad[1:-1, :-2, 1:-1] + mobility_pad[1:-1, 2:, 1:-1])
    summed = summed + 0.5 * (mobility_pad[1:-1, 1:-1, :-2] + mobility_pad[1:-1, 1:-1, 2:])
    return factor * summed


def restrict(values):
    return jnp.mean(values.reshape(values.shape[0] // 2, 2, values.shape[1] // 2, 2, values.shape[2] // 2, 2), axis=(1, 3, 5))


def prolong(values):
    expanded = jnp.broadcast_to(values[:, None, :, None, :, None],
                                (values.shape[0], 2, values.shape[1], 2, values.shape[2], 2))
    return expanded.reshape(values.shape[0] * 2, values.shape[1] * 2, values.shape[2] * 2)


def jacobi_sweep(values, rhs_value, mobility_pad, inverse, factor):
    field_pad = jnp.pad(values, ((1, 1), (1, 1), (0, 0)))
    return values + RELAXATION * (rhs_value - operate(field_pad, mobility_pad, factor)) * inverse


def reference(source, density):
    mobilities = [1.0 / density]
    for level_index in range(1, LEVELS):
        mobilities.append(restrict(mobilities[-1]))
    pads = [jnp.pad(mobility, 1, mode="edge") for mobility in mobilities]
    factors = [0.25 ** level_index for level_index in range(LEVELS)]
    inverses = [1.0 / diagonal(padded, factor) for padded, factor in zip(pads, factors)]
    sources = []
    smoothed = []
    rhs_value = source
    for level_index in range(LEVELS - 1):
        values = jnp.zeros(rhs_value.shape, rhs_value.dtype)
        for sweep_index in range(2):
            values = jacobi_sweep(values, rhs_value, pads[level_index], inverses[level_index], factors[level_index])
        residual = rhs_value - operate(jnp.pad(values, ((1, 1), (1, 1), (0, 0))), pads[level_index], factors[level_index])
        sources.append(rhs_value)
        smoothed.append(values)
        rhs_value = restrict(residual)
    coarse_pad = pads[LEVELS - 1]
    coarse_inverse = inverses[LEVELS - 1]
    coarse_factor = factors[LEVELS - 1]

    def coarse_step(sweep_index, values):
        return jacobi_sweep(values, rhs_value, coarse_pad, coarse_inverse, coarse_factor)

    values = lax.fori_loop(0, COARSE, coarse_step, jnp.zeros(rhs_value.shape, rhs_value.dtype))
    for level_index in reversed(range(LEVELS - 1)):
        values = smoothed[level_index] + prolong(values)
        for sweep_index in range(2):
            values = jacobi_sweep(values, sources[level_index], pads[level_index], inverses[level_index], factors[level_index])
    return values
```

```python
import jax
import jax.numpy as jnp
from jax import lax
from jax.experimental import pallas as pl
from jax.experimental.pallas import tpu as pltpu
from jax.sharding import PartitionSpec as P

F32 = jnp.float32
W = 24
HIGH = lax.Precision.HIGHEST


def iota(shape, dim):
    return lax.broadcasted_iota(jnp.int32, shape, dim)


def up(x):
    return pltpu.roll(x, 1, 0)


def down(x):
    return pltpu.roll(x, x.shape[0] - 1, 0)


def left(x):
    return pltpu.roll(x, 1, 1)


def right(x):
    return pltpu.roll(x, x.shape[1] - 1, 1)


def dot(a, b):
    return jnp.dot(a, b, precision=HIGH, preferred_element_type=F32)


def select_matrix(shape, where):
    return jnp.where(where(iota(shape, 0), iota(shape, 1)), 1.0, 0.0).astype(F32)


def wrap(x, n):
    return jnp.where(x < 0, x + n, jnp.where(x >= n, x - n, x))


class Level:
    def __init__(self, rows, halo, cols, right_cols, lanes, planes, nrows, ncols):
        self.rows, self.halo, self.cols, self.right_cols = rows, halo, cols, right_cols
        self.lanes, self.planes, self.nrows, self.ncols = lanes, planes, nrows, ncols
        self.total = rows + 2 * halo

    def masks(self):
        shape = (W, self.lanes)
        col = iota(shape, 0)
        col = jnp.where(col < self.cols + self.right_cols, col, col - W)
        col = wrap(col + lax.axis_index("py") * self.cols, self.ncols)
        lane = iota(shape, 1)
        return (
            lane < self.planes,
            col == 0,
            col == self.ncols - 1,
            lane == 0,
            lane == self.planes - 1,
            (lane > 0) & (lane < self.planes),
        )

    def global_row(self, i):
        return wrap(lax.axis_index("px") * self.rows - self.halo + i, self.nrows)


def prepare(level, mob, rhs, sx, sy, sz, coef, diag, out):
    inside, first_col, last_col, first_plane, last_plane, inner_plane = level.masks()

    def step(i, carry):
        m, above, below = mob[i], mob[i - 1], mob[i + 1]
        g = level.global_row(i)
        wx = m + above
        m_up, m_left = up(m), left(m)
        sx[i] = jnp.where(g == 0, 0.0, wx)
        sy[i] = jnp.where(first_col, 0.0, m + m_up)
        sz[i] = jnp.where(inner_plane, m + m_left, 0.0)
        d = 6.0 * m + jnp.where(g == 0, m, above) + jnp.where(g == level.nrows - 1, m, below)
        d = d + jnp.where(first_col, m, m_up) + jnp.where(last_col, m, down(m))
        d = d + jnp.where(first_plane, m, m_left) + jnp.where(last_plane, m, right(m))
        c = jnp.where(inside, 0.8 / d, 0.0)
        coef[i] = c
        diag[i] = d
        out[i] = c * rhs[i]
        return carry

    lax.fori_loop(1, level.total - 1, step, 0)
    last = level.total - 1
    sx[last] = jnp.where(level.global_row(last) == 0, 0.0, mob[last] + mob[last - 1])


def coupling(v, i, sx, sy, sz):
    c = v[i]
    total = sx[i] * v[i - 1] + sx[i + 1] * v[i + 1]
    wy = sy[i]
    total = total + wy * up(c) + down(wy * c)
    wz = sz[i]
    return c, total + wz * left(c) + right(wz * c)


def sweep(lo, hi, v, out, rhs, sx, sy, sz, coef):
    def step(i, carry):
        c, total = coupling(v, i, sx, sy, sz)
        out[i] = 0.2 * c + coef[i] * (rhs[i] + total)
        return carry

    lax.fori_loop(lo, hi, step, 0)


def paired_residual(pairs, lo, v, out, rhs, sx, sy, sz, diag):
    def row(i):
        c, total = coupling(v, i, sx, sy, sz)
        return rhs[i] - diag[i] * c + total

    def step(k, carry):
        i = lo + 2 * k
        out[k] = row(i) + row(i + 1)
        return carry

    lax.fori_loop(0, pairs, step, 0)


def pair_planes(lanes_in, offset=0, lanes_out=128):
    return select_matrix((lanes_in, lanes_out), lambda r, c: (r >> 1) + offset == c)


def spread_planes(lanes_out, offset=0, planes=128):
    return select_matrix((128, lanes_out), lambda r, c: ((c >> 1) + offset == r) & ((c >> 1) < planes))


def level0_kernel(lv, src, dens, lo, hi, from_left, from_right, packed, v, rhs, sx, sy, sz, coef,
                  mob, first, diag, pair, low):
    h = lv.halo
    tile = iota((8, lv.lanes), 0)

    def load(i, s, d):
        rhs[i, 0:16] = 2.0 * s
        mob[i, 0:16] = 1.0 / d
        a, b = from_right[i], from_left[i]
        rhs[i, 16:24] = 2.0 * jnp.where(tile < 4, a, b)
        mob[i, 16:24] = 1.0 / pltpu.roll(jnp.where(tile < 4, b, a), 4, 0)

    for i in range(h):
        load(i, lo[i], lo[h + i])
        load(lv.total - h + i, hi[i], hi[h + i])

    def body(i, carry):
        load(h + i, src[i], dens[i])
        return carry

    lax.fori_loop(0, lv.rows, body, 0)
    zero = jnp.zeros((W, lv.lanes), F32)
    for ref in (first, v):
        ref[0] = zero
        ref[lv.total - 1] = zero
    prepare(lv, mob, rhs, sx, sy, sz, coef, diag, first)
    sweep(1, lv.total - 1, first, v, rhs, sx, sy, sz, coef)
    half = lv.rows // 2
    z = pair_planes(lv.lanes)
    paired_residual(half, h, v, pair, rhs, sx, sy, sz, diag)

    def emit(place, scale):
        x = dot(pair[:, 0:16].reshape(half * 16, lv.lanes), z)
        low[...] = x
        y = low[pl.ds(0, half * 8, stride=2)] + low[pl.ds(1, half * 8, stride=2)]
        packed[:, place : place + 8] = (scale * y).reshape(half, 8, 128)

    emit(0, 0.5)

    def mobs(k, carry):
        pair[k] = mob[h + 2 * k] + mob[h + 2 * k + 1]
        return carry

    lax.fori_loop(0, half, mobs, 0)
    emit(8, 0.125)


def level1_kernel(lv, own, lo, hi, from_left, from_right, packed, v, rhs, sx, sy, sz, coef,
                  mob, first, diag, pair, low):
    h = lv.halo

    def load(i, block):
        rhs[i, 0:8] = block[0:8]
        mob[i, 0:8] = block[8:16]
        rhs[i, 8:16] = from_right[i, 0:8]
        mob[i, 8:16] = from_right[i, 8:16]
        rhs[i, 16:24] = from_left[i, 0:8]
        mob[i, 16:24] = from_left[i, 8:16]

    for i in range(h):
        load(i, lo[i])
        load(lv.total - h + i, hi[i])

    def body(i, carry):
        load(h + i, own[i])
        return carry

    lax.fori_loop(0, lv.rows, body, 0)
    zero = jnp.zeros((W, lv.lanes), F32)
    for ref in (first, v):
        ref[0] = zero
        ref[lv.total - 1] = zero
    prepare(lv, mob, rhs, sx, sy, sz, coef, diag, first)
    sweep(1, lv.total - 1, first, v, rhs, sx, sy, sz, coef)
    half = lv.rows // 2
    paired_residual(half, h, v, pair, rhs, sx, sy, sz, diag)
    x = 0.5 * dot(pair[...].reshape(half * W, lv.lanes), pair_planes(lv.lanes))

    def mobs(k, carry):
        pair[k] = mob[h + 2 * k] + mob[h + 2 * k + 1]
        return carry

    lax.fori_loop(0, half, mobs, 0)
    low[...] = x + 0.125 * dot(pair[...].reshape(half * W, lv.lanes), pair_planes(lv.lanes, 64))
    for k in range(half):
        a = k * W
        y = low[pl.ds(a, 8, stride=2)] + low[pl.ds(a + 1, 8, stride=2)]
        packed[k, 8:16] = y
        packed[k, 4:8] = y[0:4]
        packed[k, 0:4] = low[pl.ds(a + 16, 4, stride=2)] + low[pl.ds(a + 17, 4, stride=2)]


def level2_kernel(lv, own, lo, hi, from_left, from_right, packed, v, rhs, sx, sy, sz, coef,
                  mob, first, diag, pair, wide):
    h = lv.halo
    tile = iota((8, 128), 0)
    lane = iota((8, 128), 1) < lv.planes

    def load(i, block):
        r = pltpu.roll(from_right[i], 4, 0)
        parts = (jnp.where(tile < 4, block, r), r, from_left[i])
        for k, part in enumerate(parts):
            rhs[i, 8 * k : 8 * k + 8] = jnp.where(lane, part, 0.0)
            mob[i, 8 * k : 8 * k + 8] = jnp.where(lane, pltpu.roll(part, 64, 1), 1.0)

    for i in range(h):
        load(i, lo[i, 8:16])
        load(h + i, own[i, 8:16])
        load(2 * h + i, hi[i, 8:16])
    zero = jnp.zeros((W, lv.lanes), F32)
    for ref in (first, v):
        ref[0] = zero
        ref[lv.total - 1] = zero
    prepare(lv, mob, rhs, sx, sy, sz, coef, diag, first)
    sweep(1, lv.total - 1, first, v, rhs, sx, sy, sz, coef)
    paired_residual(8, 4, v, pair, rhs, sx, sy, sz, diag)
    for k in range(12):
        wide[k] = mob[2 * k] + mob[2 * k + 1]
    for k in range(12, 16):
        wide[k] = zero

    def column(ref, n, q):
        two = ref.reshape(n * W, 128)
        return two[pl.ds((2 * q) % W, n, stride=W)] + two[pl.ds((2 * q + 1) % W, n, stride=W)]

    f = jnp.zeros((8, 128), F32)
    m = jnp.zeros((16, 128), F32)
    for g in range(4):
        place = select_matrix((128, 128), lambda r, c: ((r >> 1) + 32 * g == c) & (r < 64))
        f = f + dot(column(pair, 8, g - 1), place)
        m = m + dot(column(wide, 16, g - 1), place)
    f, m = 0.5 * f, 0.125 * m
    p0 = select_matrix((128, 128), lambda r, c: ((r >> 1) + 96 == c) & (r < 64))
    p3 = select_matrix((128, 128), lambda r, c: ((r >> 1) == c) & (r < 64))
    beside = 0.125 * (dot(column(wide, 16, -2), p0) + dot(column(wide, 16, 3), p3))
    lanes = iota((16, 128), 1)
    nr, nc = lv.nrows // 2, lv.ncols // 2
    row = wrap(iota((16, 128), 0) - 4 + lax.axis_index("px") * 4, nr)
    col = wrap((lanes >> 5) - 1 + lax.axis_index("py") * 2, nc)
    prev = jnp.where(lanes < 32, pltpu.roll(beside, 32, 1), pltpu.roll(m, 32, 1))
    nxt = jnp.where(lanes >= 96, pltpu.roll(beside, 96, 1), pltpu.roll(m, 96, 1))
    d = 6.0 * m + jnp.where(row == 0, m, up(m)) + jnp.where(row == nr - 1, m, down(m))
    d = d + jnp.where(col == 0, m, prev) + jnp.where(col == nc - 1, m, nxt)
    plane = lanes & 31
    d = d + jnp.where(plane == 0, m, left(m)) + jnp.where(plane == 31, m, right(m))
    packed[0] = f
    packed[1] = m[2:10]
    packed[2] = (0.8 / d)[2:10]


def coarse_solve(groups, nr, nc, out):
    shape = (W, 128)
    lane = iota(shape, 1)
    row_ok = wrap(iota(shape, 0) - 10 + lax.axis_index("px") * 4, nr) > 0
    plane_ok = (lane & 31) > 0
    low, high = lane < 32, lane >= 96
    n = len(groups)
    f = [g[0] for g in groups]
    m = [g[1] for g in groups]
    c = [g[2] for g in groups]
    col_ok = [wrap((lane >> 5) - 9 + 4 * k + lax.axis_index("py") * 2, nc) > 0 for k in range(n)]
    zero = jnp.zeros(shape, F32)

    def before(x, k):
        a = pltpu.roll(x[k], 32, 1)
        b = pltpu.roll(x[k - 1], 32, 1) if k else zero
        return jnp.where(low, b, a)

    def after(x, k):
        a = pltpu.roll(x[k], 96, 1)
        b = pltpu.roll(x[k + 1], 96, 1) if k + 1 < n else zero
        return jnp.where(high, b, a)

    sx = [jnp.where(row_ok, a + up(a), 0.0) for a in m]
    sy = [jnp.where(col_ok[k], a + before(m, k), 0.0) for k, a in enumerate(m)]
    sz = [jnp.where(plane_ok, a + left(a), 0.0) for a in m]
    v = [a * b for a, b in zip(c, f)]
    for _ in range(7):
        wy = [a * b for a, b in zip(sy, v)]
        new = []
        for k in range(n):
            x = v[k]
            total = f[k] + sx[k] * up(x) + down(sx[k] * x)
            total = total + sy[k] * before(v, k) + after(wy, k)
            total = total + sz[k] * left(x) + right(sz[k] * x)
            new.append(0.2 * x + c[k] * total)
        v = new
    for k in range(n):
        out[k] = v[k]


def ascent_kernel(levels, g0, g1, g2, g3, g4, *refs):
    fields = [refs[6 * k : 6 * k + 6] for k in range(3)]
    result = refs[18]
    e3, p2, a2, b2, p1, q1, a1, b1, p0, q0, a0, b0 = refs[19:]
    lv0, lv1, lv2 = levels
    coarse_solve([g0, g1, g2, g3, g4], lv2.nrows // 2, lv2.ncols // 2, e3)

    p2[...] = jnp.zeros(p2.shape, F32)
    two = p2.reshape(8 * W, 128)
    for q in range(-2, 4):
        group, g = (q + 9) // 4, (q + 9) % 4
        spread = select_matrix((128, 128), lambda r, c: ((c >> 1) + 32 * g == r) & (c < 64))
        x = dot(e3[group, 8:16], spread)
        two[pl.ds((2 * q) % W, 8, stride=W)] = x
        two[pl.ds((2 * q + 1) % W, 8, stride=W)] = x
    v, rhs, sx, sy, sz, coef = fields[2]

    def add2(i, carry):
        a2[i] = v[i] + p2[i // 2 - 2]
        return carry

    lax.fori_loop(4, 20, add2, 0)
    sweep(5, 19, a2, b2, rhs, sx, sy, sz, coef)
    sweep(6, 18, b2, a2, rhs, sx, sy, sz, coef)

    for k in range(12):
        x = a2[k + 6]
        for s in range(2):
            p1[k, pl.ds(s, 8, stride=2)] = x[0:8]
            p1[k, pl.ds(16 + s, 4, stride=2)] = x[20:24]
    q1[...] = dot(p1[...].reshape(12 * W, 128), spread_planes(128, 0, 64)).reshape(12, W, 128)
    v1, rhs1, sx1, sy1, sz1, coef1 = fields[1]

    def add1(i, carry):
        a1[i] = v1[i] + q1[i // 2 - 1]
        return carry

    lax.fori_loop(3, 25, add1, 0)
    sweep(4, 24, a1, b1, rhs1, sx1, sy1, sz1, coef1)
    sweep(5, 23, b1, a1, rhs1, sx1, sy1, sz1, coef1)

    for k in range(18):
        x = a1[k + 5]
        for s in range(2):
            p0[k, pl.ds(s, 8, stride=2)] = x[0:8]
            p0[k, pl.ds(16 + s, 2, stride=2)] = x[8:10]
            p0[k, pl.ds(20 + s, 2, stride=2)] = x[22:24]
    q0[...] = dot(p0[...].reshape(18 * W, 128), spread_planes(256)).reshape(18, W, 256)
    v0, rhs0, sx0, sy0, sz0, coef0 = fields[0]

    def add0(i, carry):
        b0[i] = v0[i] + q0[i // 2 - 1]
        return carry

    lax.fori_loop(2, 38, add0, 0)
    sweep(3, 37, b0, a0, rhs0, sx0, sy0, sz0, coef0)

    def final(i, carry):
        c, total = coupling(a0, i, sx0, sy0, sz0)
        result[i - 4] = (0.2 * c + coef0[i] * (rhs0[i] + total))[0:16]
        return carry

    lax.fori_loop(4, 36, final, 0)


VMEM = pl.BlockSpec(memory_space=pltpu.VMEM)
LIMIT = 48 << 20


def descend(kernel, lv, inputs, packed, scratch):
    block = jax.ShapeDtypeStruct((lv.total, W, lv.lanes), F32)
    outs = pl.pallas_call(
        lambda *refs: kernel(lv, *refs),
        out_shape=[jax.ShapeDtypeStruct(packed, F32)] + [block] * 6,
        in_specs=[VMEM] * len(inputs),
        out_specs=[VMEM] * 7,
        scratch_shapes=[pltpu.VMEM(block.shape, F32)] * 3 + [pltpu.VMEM(s, F32) for s in scratch],
        compiler_params=pltpu.CompilerParams(vmem_limit_bytes=LIMIT),
        name="descent",
    )(*inputs)
    return outs[0], outs[1:]


def ring(x, axis, step):
    n = lax.axis_size(axis)
    return lax.ppermute(x, axis, [(i, (i + step) % n) for i in range(n)])


def per_device(source, density):
    npx, npy = lax.axis_size("px"), lax.axis_size("py")
    lv0 = Level(32, 4, 16, 4, 256, 256, 32 * npx, 16 * npy)
    lv1 = Level(16, 6, 8, 8, 128, 128, 16 * npx, 8 * npy)
    lv2 = Level(8, 8, 4, 8, 128, 64, 8 * npx, 4 * npy)

    h = lv0.halo
    lo = ring(jnp.concatenate([source[-h:], density[-h:]], 0), "px", 1)
    hi = ring(jnp.concatenate([source[:h], density[:h]], 0), "px", -1)
    es = lambda a, b: jnp.concatenate([lo[:h, a:b], source[:, a:b], hi[:h, a:b]], 0)
    ed = lambda a, b: jnp.concatenate([lo[h:, a:b], density[:, a:b], hi[h:, a:b]], 0)
    from_left = ring(jnp.concatenate([ed(12, 16), es(12, 16)], 1), "py", 1)
    from_right = ring(jnp.concatenate([es(0, 4), ed(0, 4)], 1), "py", -1)
    one, saved0 = descend(
        level0_kernel, lv0, (source, density, lo, hi, from_left, from_right), (16, 16, 128),
        [(16, W, 256), (256, 128)],
    )

    h = lv1.halo
    lo = ring(one[-h:], "px", 1)
    hi = ring(one[:h], "px", -1)
    wide = jnp.concatenate([lo, one, hi], 0)
    from_left = ring(wide, "py", 1)
    from_right = ring(wide, "py", -1)
    two, saved1 = descend(
        level1_kernel, lv1, (one, lo, hi, from_left, from_right), (8, 16, 128),
        [(8, W, 128), (8 * W, 128)],
    )

    lo = ring(two, "px", 1)
    hi = ring(two, "px", -1)
    from_left = ring(jnp.concatenate([lo[:, :8], two[:, :8], hi[:, :8]], 0), "py", 1)
    from_right = ring(jnp.concatenate([lo[:, 8:], two[:, 8:], hi[:, 8:]], 0), "py", -1)
    three, saved2 = descend(
        level2_kernel, lv2, (two, lo, hi, from_left, from_right), (3, 8, 128),
        [(8, W, 128), (16, W, 128)],
    )

    wide = jnp.concatenate([ring(three, "px", 2), three, ring(three, "px", -2)], 1)
    groups = [ring(wide, "py", 4), ring(wide, "py", 2), wide, ring(wide, "py", -2), ring(wide, "py", -4)]
    inputs = (*groups, *saved0, *saved1, *saved2)
    shapes = [(5, W, 128), (8, W, 128), (24, W, 128), (24, W, 128), (12, W, 128), (12, W, 128),
              (28, W, 128), (28, W, 128), (18, W, 128), (18, W, 256), (40, W, 256),
              (40, W, 256)]
    return pl.pallas_call(
        lambda *refs: ascent_kernel((lv0, lv1, lv2), *refs),
        out_shape=jax.ShapeDtypeStruct(source.shape, F32),
        in_specs=[VMEM] * len(inputs),
        out_specs=VMEM,
        scratch_shapes=[pltpu.VMEM(s, F32) for s in shapes],
        compiler_params=pltpu.CompilerParams(vmem_limit_bytes=LIMIT),
        name="ascent",
    )(*inputs)


def solution(mesh):
    spec = P("px", "py", None)
    return jax.shard_map(
        per_device, mesh=mesh, in_specs=(spec, spec), out_specs=spec, check_vma=False
    )
```

```python
import jax
import jax.numpy as jnp
from jax import lax
from jax.experimental import pallas as pl
from jax.experimental.pallas import tpu as pltpu
from jax.sharding import PartitionSpec as P

F32 = jnp.float32
W = 24
BF16 = jnp.bfloat16
UNROLL = 2


def iota(shape, dim):
    return lax.broadcasted_iota(jnp.int32, shape, dim)


def up(x):
    return pltpu.roll(x, 1, 0)


def down(x):
    return pltpu.roll(x, x.shape[0] - 1, 0)


def left(x):
    return pltpu.roll(x, 1, 1)


def right(x):
    return pltpu.roll(x, x.shape[1] - 1, 1)


def dot(a, b):
    high = a.astype(BF16)
    rest = a - high.astype(F32)
    mid = rest.astype(BF16)
    low = (rest - mid.astype(F32)).astype(BF16)
    return sum(jnp.dot(x, b, preferred_element_type=F32) for x in (high, mid, low))


def select_matrix(shape, where):
    return jnp.where(where(iota(shape, 0), iota(shape, 1)), 1.0, 0.0).astype(BF16)


def wrap(x, n):
    return jnp.where(x < 0, x + n, jnp.where(x >= n, x - n, x))


class Level:
    def __init__(self, rows, halo, cols, right_cols, lanes, planes, nrows, ncols):
        self.rows, self.halo, self.cols, self.right_cols = rows, halo, cols, right_cols
        self.lanes, self.planes, self.nrows, self.ncols = lanes, planes, nrows, ncols
        self.total = rows + 2 * halo

    def masks(self):
        shape = (W, self.lanes)
        col = iota(shape, 0)
        col = jnp.where(col < self.cols + self.right_cols, col, col - W)
        col = wrap(col + lax.axis_index("py") * self.cols, self.ncols)
        lane = iota(shape, 1)
        edge = lambda hit: jnp.where(hit, 2.0, 0.0)
        extra = edge(col == 0) + edge(col == self.ncols - 1)
        extra = extra + edge(lane == 0) + edge(lane == self.planes - 1)
        return lane < self.planes, col > 0, (lane > 0) & (lane < self.planes), extra

    def global_row(self, i):
        return wrap(lax.axis_index("px") * self.rows - self.halo + i, self.nrows)


def prepare(level, mob, rhs, sx, sy, sz, coef, diag, out):
    inside, inner_col, inner_plane, extra = level.masks()

    def face(i, a, b):
        return (a + b) * jnp.where(level.global_row(i) == 0, 0.0, 1.0)

    def step(i, carry):
        m, wx = carry
        below = mob[i + 1]
        g = level.global_row(i)
        next_wx = face(i + 1, m, below)
        wy = jnp.where(inner_col, m + up(m), 0.0)
        wz = jnp.where(inner_plane, m + left(m), 0.0)
        sx[i + 1] = next_wx
        sy[i] = wy
        sz[i] = wz
        ends = jnp.where((g == 0) | (g == level.nrows - 1), 2.0, 0.0)
        d = (wx + next_wx) + (wy + down(wy)) + (wz + right(wz)) + (extra + ends) * m
        c = 0.8 / d
        if level.planes < level.lanes:
            c = jnp.where(inside, c, 0.0)
        coef[i] = c
        diag[i] = d
        out[i] = c * rhs[i]
        return below, next_wx

    first = face(1, mob[0], mob[1])
    sx[1] = first
    lax.fori_loop(1, level.total - 1, step, (mob[1], first), unroll=UNROLL)


def walk(lo, hi, load, emit, sx, sy, sz):
    def step(i, carry):
        above, c, wx = carry
        below, next_wx = load(i + 1), sx[i + 1]
        wy, wz = sy[i], sz[i]
        total = (wx * above + next_wx * below) + (wy * up(c) + down(wy * c))
        total = total + (wz * left(c) + right(wz * c))
        emit(i, c, total)
        return c, below, next_wx

    lax.fori_loop(lo, hi, step, (load(lo - 1), load(lo), sx[lo]), unroll=UNROLL)


def sweep(lo, hi, load, store, rhs, sx, sy, sz, coef):
    def emit(i, c, total):
        store(i, 0.2 * c + coef[i] * (rhs[i] + total))

    walk(lo, hi, load, emit, sx, sy, sz)


def reader(ref):
    return lambda i: ref[i]


def writer(ref):
    def store(i, x):
        ref[i] = x

    return store


def paired_residual(pairs, lo, cols, v, out, rhs, sx, sy, sz, diag):
    def step(k, carry):
        above, c, wx = carry
        done = []
        for j in range(2):
            i = lo + 2 * k + j
            below, next_wx = v[i + 1], sx[i + 1]
            wy, wz = sy[i], sz[i]
            total = (wx * above + next_wx * below) + (wy * up(c) + down(wy * c))
            total = total + (wz * left(c) + right(wz * c))
            done.append((rhs[i] - diag[i] * c + total)[0:cols])
            above, c, wx = c, below, next_wx
        out[k] = done[0] + done[1]
        return above, c, wx

    lax.fori_loop(0, pairs, step, (v[lo - 1], v[lo], sx[lo]))


def pair_planes(lanes_in, offset=0, lanes_out=128):
    return select_matrix((lanes_in, lanes_out), lambda r, c: (r >> 1) + offset == c)


def spread_planes(lanes_out, offset=0, planes=128):
    return select_matrix((128, lanes_out), lambda r, c: ((c >> 1) + offset == r) & ((c >> 1) < planes))


def level0_kernel(lv, src, dens, lo, hi, from_left, from_right, corner_left, corner_right, packed, v, rhs, sx, sy, sz, coef,
                  mob, first, diag, pair, low):
    h = lv.halo
    tile = iota((8, lv.lanes), 0)

    def load(i, s, d, a, b):
        rhs[i, 0:16] = 2.0 * s
        mob[i, 0:16] = 1.0 / d
        rhs[i, 16:24] = 2.0 * jnp.where(tile < 4, a, b)
        mob[i, 16:24] = 1.0 / pltpu.roll(jnp.where(tile < 4, b, a), 4, 0)

    for i in range(h):
        load(i, lo[i], lo[h + i], corner_right[i], corner_left[i])
        load(lv.total - h + i, hi[i], hi[h + i], corner_right[h + i], corner_left[h + i])

    def body(i, carry):
        load(h + i, src[i], dens[i], from_right[i], from_left[i])
        return carry

    lax.fori_loop(0, lv.rows, body, 0, unroll=UNROLL)
    zero = jnp.zeros((W, lv.lanes), F32)
    for ref in (first, v):
        ref[0] = zero
        ref[lv.total - 1] = zero
    prepare(lv, mob, rhs, sx, sy, sz, coef, diag, first)
    sweep(1, lv.total - 1, reader(first), writer(v), rhs, sx, sy, sz, coef)
    half = lv.rows // 2
    z = pair_planes(lv.lanes)
    paired_residual(half, h, 16, v, pair.at[:, 0:16], rhs, sx, sy, sz, diag)

    low[0 : half * 16] = 0.5 * dot(pair[:, 0:16].reshape(half * 16, lv.lanes), z)
    fine = low[pl.ds(0, half * 8, stride=2)] + low[pl.ds(1, half * 8, stride=2)]

    def mobs(k, carry):
        pair[k] = mob[h + 2 * k] + mob[h + 2 * k + 1]
        return carry

    lax.fori_loop(0, half, mobs, 0, unroll=UNROLL)
    low[...] = 0.125 * dot(pair[...].reshape(half * W, lv.lanes), z)
    at = iota((8, 128), 0)
    beside = jnp.zeros((4, 128), F32)
    for k in range(half):
        f = fine[8 * k : 8 * k + 8]
        m = low[pl.ds(k * W, 8, stride=2)] + low[pl.ds(k * W + 1, 8, stride=2)]
        e = low[pl.ds(k * W + 16, 4, stride=2)] + low[pl.ds(k * W + 17, 4, stride=2)]
        e = pltpu.roll(jnp.concatenate([e, beside], 0), 2, 0)
        shifted = pltpu.roll(m, 2, 0)
        packed[k, 0:8] = jnp.where(at < 4, pltpu.roll(f, 4, 0), shifted)
        packed[k, 8:16] = jnp.where(at < 4, f, shifted)
        packed[k, 16:24] = jnp.where((at < 2) | (at >= 6), m, e)


def level1_kernel(lv, own, lo, hi, from_left, from_right, packed, v, rhs, sx, sy, sz, coef,
                  mob, first, diag, pair, low):
    h = lv.halo

    at = iota((8, lv.lanes), 0)

    def load(i, block):
        t0, t1, t2 = block[0:8], block[8:16], block[16:24]
        a, b = from_right[i], from_left[i]
        rhs[i, 0:8] = jnp.where(at < 4, t1, pltpu.roll(t0, 4, 0))
        rhs[i, 8:16] = a
        rhs[i, 16:24] = pltpu.roll(b, 4, 0)
        mob[i, 0:8] = jnp.where((at < 2) | (at >= 6), t2, pltpu.roll(t0, 6, 0))
        far = jnp.where(at < 6, pltpu.roll(a, 6, 0), 1.0)
        mob[i, 8:16] = jnp.where(at < 2, pltpu.roll(t2, 6, 0), far)
        far = jnp.where(at < 2, 1.0, pltpu.roll(b, 6, 0))
        mob[i, 16:24] = jnp.where(at < 6, far, pltpu.roll(t2, 2, 0))

    for i in range(h):
        load(i, lo[i])
        load(lv.total - h + i, hi[i])

    def body(i, carry):
        load(h + i, own[i])
        return carry

    lax.fori_loop(0, lv.rows, body, 0, unroll=UNROLL)
    zero = jnp.zeros((W, lv.lanes), F32)
    for ref in (first, v):
        ref[0] = zero
        ref[lv.total - 1] = zero
    prepare(lv, mob, rhs, sx, sy, sz, coef, diag, first)
    sweep(1, lv.total - 1, reader(first), writer(v), rhs, sx, sy, sz, coef)
    half = lv.rows // 2
    paired_residual(half, h, W, v, pair, rhs, sx, sy, sz, diag)
    x = 0.5 * dot(pair[...].reshape(half * W, lv.lanes), pair_planes(lv.lanes))

    def mobs(k, carry):
        pair[k] = mob[h + 2 * k] + mob[h + 2 * k + 1]
        return carry

    lax.fori_loop(0, half, mobs, 0)
    low[...] = x + 0.125 * dot(pair[...].reshape(half * W, lv.lanes), pair_planes(lv.lanes, 64))
    for k in range(half):
        a = k * W
        y = low[pl.ds(a, 8, stride=2)] + low[pl.ds(a + 1, 8, stride=2)]
        packed[k, 8:16] = y
        packed[k, 4:8] = y[0:4]
        packed[k, 0:4] = low[pl.ds(a + 16, 4, stride=2)] + low[pl.ds(a + 17, 4, stride=2)]


def level2_kernel(lv, own, lo, hi, from_left, from_right, packed, v, rhs, sx, sy, sz, coef,
                  mob, first, diag, pair, wide):
    h = lv.halo
    tile = iota((8, 128), 0)
    lane = iota((8, 128), 1) < lv.planes

    def load(i, block):
        r = pltpu.roll(from_right[i], 4, 0)
        parts = (jnp.where(tile < 4, block, r), r, from_left[i])
        for k, part in enumerate(parts):
            rhs[i, 8 * k : 8 * k + 8] = jnp.where(lane, part, 0.0)
            mob[i, 8 * k : 8 * k + 8] = jnp.where(lane, pltpu.roll(part, 64, 1), 1.0)

    for i in range(h):
        load(i, lo[i, 8:16])
        load(h + i, own[i, 8:16])
        load(2 * h + i, hi[i, 8:16])
    zero = jnp.zeros((W, lv.lanes), F32)
    for ref in (first, v):
        ref[0] = zero
        ref[lv.total - 1] = zero
    prepare(lv, mob, rhs, sx, sy, sz, coef, diag, first)
    sweep(1, lv.total - 1, reader(first), writer(v), rhs, sx, sy, sz, coef)
    paired_residual(8, 4, W, v, pair, rhs, sx, sy, sz, diag)
    for k in range(12):
        wide[k] = mob[2 * k] + mob[2 * k + 1]
    for k in range(12, 16):
        wide[k] = zero

    def column(ref, n, q):
        two = ref.reshape(n * W, 128)
        return two[pl.ds((2 * q) % W, n, stride=W)] + two[pl.ds((2 * q + 1) % W, n, stride=W)]

    f = jnp.zeros((8, 128), F32)
    m = jnp.zeros((16, 128), F32)
    for g in range(4):
        place = select_matrix((128, 128), lambda r, c: ((r >> 1) + 32 * g == c) & (r < 64))
        f = f + dot(column(pair, 8, g - 1), place)
        m = m + dot(column(wide, 16, g - 1), place)
    f, m = 0.5 * f, 0.125 * m
    p0 = select_matrix((128, 128), lambda r, c: ((r >> 1) + 96 == c) & (r < 64))
    p3 = select_matrix((128, 128), lambda r, c: ((r >> 1) == c) & (r < 64))
    beside = 0.125 * (dot(column(wide, 16, -2), p0) + dot(column(wide, 16, 3), p3))
    lanes = iota((16, 128), 1)
    nr, nc = lv.nrows // 2, lv.ncols // 2
    row = wrap(iota((16, 128), 0) - 4 + lax.axis_index("px") * 4, nr)
    col = wrap((lanes >> 5) - 1 + lax.axis_index("py") * 2, nc)
    prev = jnp.where(lanes < 32, pltpu.roll(beside, 32, 1), pltpu.roll(m, 32, 1))
    nxt = jnp.where(lanes >= 96, pltpu.roll(beside, 96, 1), pltpu.roll(m, 96, 1))
    d = 6.0 * m + jnp.where(row == 0, m, up(m)) + jnp.where(row == nr - 1, m, down(m))
    d = d + jnp.where(col == 0, m, prev) + jnp.where(col == nc - 1, m, nxt)
    plane = lanes & 31
    d = d + jnp.where(plane == 0, m, left(m)) + jnp.where(plane == 31, m, right(m))
    packed[0] = f
    packed[1] = m[2:10]
    packed[2] = (0.8 / d)[2:10]


def coarse_solve(groups, nr, nc, out):
    shape = (W, 128)
    lane = iota(shape, 1)
    row_ok = wrap(iota(shape, 0) - 10 + lax.axis_index("px") * 4, nr) > 0
    plane_ok = (lane & 31) > 0
    low, high = lane < 32, lane >= 96
    n = len(groups)
    f = [g[0] for g in groups]
    m = [g[1] for g in groups]
    c = [g[2] for g in groups]
    col_ok = [wrap((lane >> 5) - 9 + 4 * k + lax.axis_index("py") * 2, nc) > 0 for k in range(n)]
    zero = jnp.zeros(shape, F32)

    def before(x, k):
        a = pltpu.roll(x[k], 32, 1)
        b = pltpu.roll(x[k - 1], 32, 1) if k else zero
        return jnp.where(low, b, a)

    def after(x, k):
        a = pltpu.roll(x[k], 96, 1)
        b = pltpu.roll(x[k + 1], 96, 1) if k + 1 < n else zero
        return jnp.where(high, b, a)

    sx = [jnp.where(row_ok, a + up(a), 0.0) for a in m]
    sy = [jnp.where(col_ok[k], a + before(m, k), 0.0) for k, a in enumerate(m)]
    sz = [jnp.where(plane_ok, a + left(a), 0.0) for a in m]
    v = [a * b for a, b in zip(c, f)]
    for _ in range(7):
        wy = [a * b for a, b in zip(sy, v)]
        new = []
        for k in range(n):
            x = v[k]
            total = f[k] + sx[k] * up(x) + down(sx[k] * x)
            total = total + sy[k] * before(v, k) + after(wy, k)
            total = total + sz[k] * left(x) + right(sz[k] * x)
            new.append(0.2 * x + c[k] * total)
        v = new
    for k in range(n):
        out[k] = v[k]


def ascent_kernel(levels, g0, g1, g2, g3, g4, *refs):
    fields = [refs[6 * k : 6 * k + 6] for k in range(3)]
    result = refs[18]
    e3, p2, a2, b2, p1, q1, a1, b1, p0, q0, a0 = refs[19:]
    lv0, lv1, lv2 = levels
    coarse_solve([g0, g1, g2, g3, g4], lv2.nrows // 2, lv2.ncols // 2, e3)

    p2[...] = jnp.zeros(p2.shape, F32)
    two = p2.reshape(8 * W, 128)
    for q in range(-2, 4):
        group, g = (q + 9) // 4, (q + 9) % 4
        spread = select_matrix((128, 128), lambda r, c: ((c >> 1) + 32 * g == r) & (c < 64))
        x = dot(e3[group, 8:16], spread)
        two[pl.ds((2 * q) % W, 8, stride=W)] = x
        two[pl.ds((2 * q + 1) % W, 8, stride=W)] = x
    v, rhs, sx, sy, sz, coef = fields[2]

    value2 = lambda i: v[i] + p2[i // 2 - 2]
    sweep(5, 19, value2, writer(b2), rhs, sx, sy, sz, coef)
    sweep(6, 18, reader(b2), writer(a2), rhs, sx, sy, sz, coef)

    for k in range(12):
        x = a2[k + 6]
        for s in range(2):
            p1[k, pl.ds(s, 8, stride=2)] = x[0:8]
            p1[k, pl.ds(16 + s, 4, stride=2)] = x[20:24]
    q1[...] = dot(p1[...].reshape(12 * W, 128), spread_planes(128, 0, 64)).reshape(12, W, 128)
    v1, rhs1, sx1, sy1, sz1, coef1 = fields[1]

    value1 = lambda i: v1[i] + q1[i // 2 - 1]
    sweep(4, 24, value1, writer(b1), rhs1, sx1, sy1, sz1, coef1)
    sweep(5, 23, reader(b1), writer(a1), rhs1, sx1, sy1, sz1, coef1)

    for k in range(18):
        x = a1[k + 5]
        for s in range(2):
            p0[k, pl.ds(s, 8, stride=2)] = x[0:8]
            p0[k, pl.ds(16 + s, 2, stride=2)] = x[8:10]
            p0[k, pl.ds(20 + s, 2, stride=2)] = x[22:24]
    q0[...] = dot(p0[...].reshape(18 * W, 128), spread_planes(256)).reshape(18, W, 256)
    v0, rhs0, sx0, sy0, sz0, coef0 = fields[0]

    value0 = lambda i: v0[i] + q0[i // 2 - 1]
    sweep(3, 37, value0, writer(a0), rhs0, sx0, sy0, sz0, coef0)

    def final(i, x):
        result[i - 4] = x[0:16]

    sweep(4, 36, reader(a0), final, rhs0, sx0, sy0, sz0, coef0)


VMEM = pl.BlockSpec(memory_space=pltpu.VMEM)
LIMIT = 14 << 20


def descend(kernel, lv, inputs, packed, scratch):
    block = jax.ShapeDtypeStruct((lv.total, W, lv.lanes), F32)
    outs = pl.pallas_call(
        lambda *refs: kernel(lv, *refs),
        out_shape=[jax.ShapeDtypeStruct(packed, F32)] + [block] * 6,
        in_specs=[VMEM] * len(inputs),
        out_specs=[VMEM] * 7,
        scratch_shapes=[pltpu.VMEM(block.shape, F32)] * 3 + [pltpu.VMEM(s, F32) for s in scratch],
        compiler_params=pltpu.CompilerParams(vmem_limit_bytes=LIMIT),
        name="descent",
    )(*inputs)
    return outs[0], outs[1:]


def ring(x, axis, step):
    n = lax.axis_size(axis)
    return lax.ppermute(x, axis, [(i, (i + step) % n) for i in range(n)])


def per_device(source, density):
    npx, npy = lax.axis_size("px"), lax.axis_size("py")
    lv0 = Level(32, 4, 16, 4, 256, 256, 32 * npx, 16 * npy)
    lv1 = Level(16, 6, 8, 8, 128, 128, 16 * npx, 8 * npy)
    lv2 = Level(8, 8, 4, 8, 128, 64, 8 * npx, 4 * npy)

    h = lv0.halo
    lo = ring(jnp.concatenate([source[-h:], density[-h:]], 0), "px", 1)
    hi = ring(jnp.concatenate([source[:h], density[:h]], 0), "px", -1)
    to_right = lambda s, d: jnp.concatenate([d[:, 12:16], s[:, 12:16]], 1)
    to_left = lambda s, d: jnp.concatenate([s[:, 0:4], d[:, 0:4]], 1)
    from_left = ring(to_right(source, density), "py", 1)
    from_right = ring(to_left(source, density), "py", -1)
    row_source = jnp.concatenate([lo[:h], hi[:h]], 0)
    row_density = jnp.concatenate([lo[h:], hi[h:]], 0)
    corner_left = ring(to_right(row_source, row_density), "py", 1)
    corner_right = ring(to_left(row_source, row_density), "py", -1)
    one, saved0 = descend(
        level0_kernel, lv0, (source, density, lo, hi, from_left, from_right, corner_left, corner_right),
        (16, W, 128),
        [(16, W, 256), (16 * W, 128)],
    )

    h = lv1.halo
    lo = ring(one[-h:], "px", 1)
    hi = ring(one[:h], "px", -1)
    wide = lambda a: jnp.concatenate([lo[:, a : a + 8], one[:, a : a + 8], hi[:, a : a + 8]], 0)
    from_left = ring(wide(0), "py", 1)
    from_right = ring(wide(8), "py", -1)
    two, saved1 = descend(
        level1_kernel, lv1, (one, lo, hi, from_left, from_right), (8, 16, 128),
        [(8, W, 128), (8 * W, 128)],
    )

    lo = ring(two, "px", 1)
    hi = ring(two, "px", -1)
    from_left = ring(jnp.concatenate([lo[:, :8], two[:, :8], hi[:, :8]], 0), "py", 1)
    from_right = ring(jnp.concatenate([lo[:, 8:], two[:, 8:], hi[:, 8:]], 0), "py", -1)
    three, saved2 = descend(
        level2_kernel, lv2, (two, lo, hi, from_left, from_right), (3, 8, 128),
        [(8, W, 128), (16, W, 128)],
    )

    wide = jnp.concatenate([ring(three, "px", 2), three, ring(three, "px", -2)], 1)
    groups = [ring(wide, "py", 4), ring(wide, "py", 2), wide, ring(wide, "py", -2), ring(wide, "py", -4)]
    inputs = (*groups, *saved0, *saved1, *saved2)
    shapes = [(5, W, 128), (8, W, 128), (24, W, 128), (24, W, 128), (12, W, 128), (12, W, 128),
              (28, W, 128), (28, W, 128), (18, W, 128), (18, W, 256), (40, W, 256)]
    return pl.pallas_call(
        lambda *refs: ascent_kernel((lv0, lv1, lv2), *refs),
        out_shape=jax.ShapeDtypeStruct(source.shape, F32),
        in_specs=[VMEM] * len(inputs),
        out_specs=VMEM,
        scratch_shapes=[pltpu.VMEM(s, F32) for s in shapes],
        compiler_params=pltpu.CompilerParams(vmem_limit_bytes=LIMIT),
        name="ascent",
    )(*inputs)


def solution(mesh):
    spec = P("px", "py", None)
    return jax.shard_map(
        per_device, mesh=mesh, in_specs=(spec, spec), out_specs=spec, check_vma=False
    )
```

```python
import jax
import jax.numpy as jnp
from jax import lax
from jax.experimental import pallas as pl
from jax.experimental.pallas import tpu as pltpu
from jax.sharding import PartitionSpec as P

F32 = jnp.float32
W = 24
BF16 = jnp.bfloat16
UNROLL = 2


def iota(shape, dim):
    return lax.broadcasted_iota(jnp.int32, shape, dim)


def up(x):
    return pltpu.roll(x, 1, 0)


def down(x):
    return pltpu.roll(x, x.shape[0] - 1, 0)


def left(x):
    return pltpu.roll(x, 1, 1)


def right(x):
    return pltpu.roll(x, x.shape[1] - 1, 1)


def dot(a, b):
    high = a.astype(BF16)
    rest = a - high.astype(F32)
    mid = rest.astype(BF16)
    low = (rest - mid.astype(F32)).astype(BF16)
    return sum(jnp.dot(x, b, preferred_element_type=F32) for x in (high, mid, low))


def select_matrix(shape, where):
    return jnp.where(where(iota(shape, 0), iota(shape, 1)), 1.0, 0.0).astype(BF16)


def wrap(x, n):
    return jnp.where(x < 0, x + n, jnp.where(x >= n, x - n, x))


class Level:
    def __init__(self, rows, halo, cols, right_cols, lanes, planes, nrows, ncols):
        self.rows, self.halo, self.cols, self.right_cols = rows, halo, cols, right_cols
        self.lanes, self.planes, self.nrows, self.ncols = lanes, planes, nrows, ncols
        self.total = rows + 2 * halo

    def masks(self):
        shape = (W, self.lanes)
        col = iota(shape, 0)
        col = jnp.where(col < self.cols + self.right_cols, col, col - W)
        col = wrap(col + lax.axis_index("py") * self.cols, self.ncols)
        lane = iota(shape, 1)
        edge = lambda hit: jnp.where(hit, 2.0, 0.0)
        extra = edge(col == 0) + edge(col == self.ncols - 1)
        extra = extra + edge(lane == 0) + edge(lane == self.planes - 1)
        return lane < self.planes, col > 0, (lane > 0) & (lane < self.planes), extra

    def global_row(self, i):
        return wrap(lax.axis_index("px") * self.rows - self.halo + i, self.nrows)


def prepare(level, mob, rhs, sx, sy, sz, coef, diag, out):
    inside, inner_col, inner_plane, extra = level.masks()

    def face(i, a, b):
        return (a + b) * jnp.where(level.global_row(i) == 0, 0.0, 1.0)

    def step(i, carry):
        m, wx = carry
        below = mob[i + 1]
        g = level.global_row(i)
        next_wx = face(i + 1, m, below)
        wy = jnp.where(inner_col, m + up(m), 0.0)
        wz = jnp.where(inner_plane, m + left(m), 0.0)
        sx[i + 1] = next_wx
        sy[i] = wy
        sz[i] = wz
        ends = jnp.where((g == 0) | (g == level.nrows - 1), 2.0, 0.0)
        d = (wx + next_wx) + (wy + down(wy)) + (wz + right(wz)) + (extra + ends) * m
        c = 0.8 / d
        if level.planes < level.lanes:
            c = jnp.where(inside, c, 0.0)
        coef[i] = c
        diag[i] = d
        out[i] = c * rhs[i]
        return below, next_wx

    first = face(1, mob[0], mob[1])
    sx[1] = first
    lax.fori_loop(1, level.total - 1, step, (mob[1], first), unroll=UNROLL)


def walk(lo, hi, load, emit, sx, sy, sz):
    def step(i, carry):
        above, c, wx = carry
        below, next_wx = load(i + 1), sx[i + 1]
        wy, wz = sy[i], sz[i]
        total = (wx * above + next_wx * below) + (wy * up(c) + down(wy * c))
        total = total + (wz * left(c) + right(wz * c))
        emit(i, c, total)
        return c, below, next_wx

    lax.fori_loop(lo, hi, step, (load(lo - 1), load(lo), sx[lo]), unroll=UNROLL)


def sweep(lo, hi, load, store, rhs, sx, sy, sz, coef):
    def emit(i, c, total):
        store(i, 0.2 * c + coef[i] * (rhs[i] + total))

    walk(lo, hi, load, emit, sx, sy, sz)


def reader(ref):
    return lambda i: ref[i]


def writer(ref):
    def store(i, x):
        ref[i] = x

    return store


def paired_residual(pairs, lo, cols, v, out, rhs, sx, sy, sz, diag):
    def step(k, carry):
        above, c, wx = carry
        done = []
        for j in range(2):
            i = lo + 2 * k + j
            below, next_wx = v[i + 1], sx[i + 1]
            wy, wz = sy[i], sz[i]
            total = (wx * above + next_wx * below) + (wy * up(c) + down(wy * c))
            total = total + (wz * left(c) + right(wz * c))
            done.append((rhs[i] - diag[i] * c + total)[0:cols])
            above, c, wx = c, below, next_wx
        out[k] = done[0] + done[1]
        return above, c, wx

    lax.fori_loop(0, pairs, step, (v[lo - 1], v[lo], sx[lo]))


def pair_planes(lanes_in, offset=0, lanes_out=128):
    return select_matrix((lanes_in, lanes_out), lambda r, c: (r >> 1) + offset == c)


def spread_planes(lanes_out, offset=0, planes=128):
    return select_matrix((128, lanes_out), lambda r, c: ((c >> 1) + offset == r) & ((c >> 1) < planes))


def chooser(axis, step=1):
    odd = is_odd(axis, step)
    return lambda a, b: (jnp.where(odd, a, b), jnp.where(odd, b, a))


def halo_readers(rows0, rows1):
    choose = chooser("px")
    lo = lambda i: choose(rows0[i], rows1[i])[0]
    hi = lambda i: choose(rows0[i], rows1[i])[1]
    return lo, hi, chooser("py")


def level0_kernel(lv, src, dens, rows0, rows1, sides0, sides1, corners0, corners1, packed, v, rhs, sx, sy, sz, coef,
                  mob, first, diag, pair, low):
    h = lv.halo
    tile = iota((8, lv.lanes), 0)
    lo, hi, choose = halo_readers(rows0, rows1)

    def load(i, s, d, a, b):
        rhs[i, 0:16] = 2.0 * s
        mob[i, 0:16] = 1.0 / d
        rhs[i, 16:24] = 2.0 * jnp.where(tile < 4, a, b)
        mob[i, 16:24] = 1.0 / pltpu.roll(jnp.where(tile < 4, b, a), 4, 0)

    for i in range(h):
        left_side, right_side = choose(corners0[i], corners1[i])
        load(i, lo(i), lo(h + i), right_side, left_side)
        left_side, right_side = choose(corners0[h + i], corners1[h + i])
        load(lv.total - h + i, hi(i), hi(h + i), right_side, left_side)

    def body(i, carry):
        left_side, right_side = choose(sides0[i], sides1[i])
        load(h + i, src[i], dens[i], right_side, left_side)
        return carry

    lax.fori_loop(0, lv.rows, body, 0, unroll=UNROLL)
    zero = jnp.zeros((W, lv.lanes), F32)
    for ref in (first, v):
        ref[0] = zero
        ref[lv.total - 1] = zero
    prepare(lv, mob, rhs, sx, sy, sz, coef, diag, first)
    sweep(1, lv.total - 1, reader(first), writer(v), rhs, sx, sy, sz, coef)
    half = lv.rows // 2
    z = pair_planes(lv.lanes)
    paired_residual(half, h, 16, v, pair.at[:, 0:16], rhs, sx, sy, sz, diag)

    low[0 : half * 16] = 0.5 * dot(pair[:, 0:16].reshape(half * 16, lv.lanes), z)
    fine = low[pl.ds(0, half * 8, stride=2)] + low[pl.ds(1, half * 8, stride=2)]

    def mobs(k, carry):
        pair[k] = mob[h + 2 * k] + mob[h + 2 * k + 1]
        return carry

    lax.fori_loop(0, half, mobs, 0, unroll=UNROLL)
    low[...] = 0.125 * dot(pair[...].reshape(half * W, lv.lanes), z)
    at = iota((8, 128), 0)
    beside = jnp.zeros((4, 128), F32)
    for k in range(half):
        f = fine[8 * k : 8 * k + 8]
        m = low[pl.ds(k * W, 8, stride=2)] + low[pl.ds(k * W + 1, 8, stride=2)]
        e = low[pl.ds(k * W + 16, 4, stride=2)] + low[pl.ds(k * W + 17, 4, stride=2)]
        e = pltpu.roll(jnp.concatenate([e, beside], 0), 2, 0)
        shifted = pltpu.roll(m, 2, 0)
        packed[k, 0:8] = jnp.where(at < 4, pltpu.roll(f, 4, 0), shifted)
        packed[k, 8:16] = jnp.where(at < 4, f, shifted)
        packed[k, 16:24] = jnp.where((at < 2) | (at >= 6), m, e)


def level1_kernel(lv, own, rows0, rows1, sides0, sides1, packed, v, rhs, sx, sy, sz, coef,
                  mob, first, diag, pair, low):
    h = lv.halo

    at = iota((8, lv.lanes), 0)
    lo, hi, choose = halo_readers(rows0, rows1)

    def load(i, block):
        t0, t1, t2 = block[0:8], block[8:16], block[16:24]
        b, a = choose(sides0[i], sides1[i])
        rhs[i, 0:8] = jnp.where(at < 4, t1, pltpu.roll(t0, 4, 0))
        rhs[i, 8:16] = a
        rhs[i, 16:24] = pltpu.roll(b, 4, 0)
        mob[i, 0:8] = jnp.where((at < 2) | (at >= 6), t2, pltpu.roll(t0, 6, 0))
        far = jnp.where(at < 6, pltpu.roll(a, 6, 0), 1.0)
        mob[i, 8:16] = jnp.where(at < 2, pltpu.roll(t2, 6, 0), far)
        far = jnp.where(at < 2, 1.0, pltpu.roll(b, 6, 0))
        mob[i, 16:24] = jnp.where(at < 6, far, pltpu.roll(t2, 2, 0))

    for i in range(h):
        load(i, lo(i))
        load(lv.total - h + i, hi(i))

    def body(i, carry):
        load(h + i, own[i])
        return carry

    lax.fori_loop(0, lv.rows, body, 0, unroll=UNROLL)
    zero = jnp.zeros((W, lv.lanes), F32)
    for ref in (first, v):
        ref[0] = zero
        ref[lv.total - 1] = zero
    prepare(lv, mob, rhs, sx, sy, sz, coef, diag, first)
    sweep(1, lv.total - 1, reader(first), writer(v), rhs, sx, sy, sz, coef)
    half = lv.rows // 2
    paired_residual(half, h, W, v, pair, rhs, sx, sy, sz, diag)
    x = 0.5 * dot(pair[...].reshape(half * W, lv.lanes), pair_planes(lv.lanes))

    def mobs(k, carry):
        pair[k] = mob[h + 2 * k] + mob[h + 2 * k + 1]
        return carry

    lax.fori_loop(0, half, mobs, 0)
    low[...] = x + 0.125 * dot(pair[...].reshape(half * W, lv.lanes), pair_planes(lv.lanes, 64))
    for k in range(half):
        a = k * W
        y = low[pl.ds(a, 8, stride=2)] + low[pl.ds(a + 1, 8, stride=2)]
        packed[k, 8:16] = y
        packed[k, 4:8] = y[0:4]
        packed[k, 0:4] = low[pl.ds(a + 16, 4, stride=2)] + low[pl.ds(a + 17, 4, stride=2)]


def level2_kernel(lv, own, rows0, rows1, sides0, sides1, packed, v, rhs, sx, sy, sz, coef,
                  mob, first, diag, pair, wide):
    h = lv.halo
    tile = iota((8, 128), 0)
    lane = iota((8, 128), 1) < lv.planes
    lo, hi, choose = halo_readers(rows0, rows1)

    def load(i, block):
        l, r = choose(sides0[i], sides1[i])
        r = pltpu.roll(r, 4, 0)
        parts = (jnp.where(tile < 4, block, r), r, l)
        for k, part in enumerate(parts):
            rhs[i, 8 * k : 8 * k + 8] = jnp.where(lane, part, 0.0)
            mob[i, 8 * k : 8 * k + 8] = jnp.where(lane, pltpu.roll(part, 64, 1), 1.0)

    for i in range(h):
        load(i, lo(i)[8:16])
        load(h + i, own[i, 8:16])
        load(2 * h + i, hi(i)[8:16])
    zero = jnp.zeros((W, lv.lanes), F32)
    for ref in (first, v):
        ref[0] = zero
        ref[lv.total - 1] = zero
    prepare(lv, mob, rhs, sx, sy, sz, coef, diag, first)
    sweep(1, lv.total - 1, reader(first), writer(v), rhs, sx, sy, sz, coef)
    paired_residual(8, 4, W, v, pair, rhs, sx, sy, sz, diag)
    for k in range(12):
        wide[k] = mob[2 * k] + mob[2 * k + 1]
    for k in range(12, 16):
        wide[k] = zero

    def column(ref, n, q):
        two = ref.reshape(n * W, 128)
        return two[pl.ds((2 * q) % W, n, stride=W)] + two[pl.ds((2 * q + 1) % W, n, stride=W)]

    f = jnp.zeros((8, 128), F32)
    m = jnp.zeros((16, 128), F32)
    for g in range(4):
        place = select_matrix((128, 128), lambda r, c: ((r >> 1) + 32 * g == c) & (r < 64))
        f = f + dot(column(pair, 8, g - 1), place)
        m = m + dot(column(wide, 16, g - 1), place)
    f, m = 0.5 * f, 0.125 * m
    p0 = select_matrix((128, 128), lambda r, c: ((r >> 1) + 96 == c) & (r < 64))
    p3 = select_matrix((128, 128), lambda r, c: ((r >> 1) == c) & (r < 64))
    beside = 0.125 * (dot(column(wide, 16, -2), p0) + dot(column(wide, 16, 3), p3))
    lanes = iota((16, 128), 1)
    nr, nc = lv.nrows // 2, lv.ncols // 2
    row = wrap(iota((16, 128), 0) - 4 + lax.axis_index("px") * 4, nr)
    col = wrap((lanes >> 5) - 1 + lax.axis_index("py") * 2, nc)
    prev = jnp.where(lanes < 32, pltpu.roll(beside, 32, 1), pltpu.roll(m, 32, 1))
    nxt = jnp.where(lanes >= 96, pltpu.roll(beside, 96, 1), pltpu.roll(m, 96, 1))
    d = 6.0 * m + jnp.where(row == 0, m, up(m)) + jnp.where(row == nr - 1, m, down(m))
    d = d + jnp.where(col == 0, m, prev) + jnp.where(col == nc - 1, m, nxt)
    plane = lanes & 31
    d = d + jnp.where(plane == 0, m, left(m)) + jnp.where(plane == 31, m, right(m))
    packed[0] = f
    packed[1] = m[2:10]
    packed[2] = (0.8 / d)[2:10]


def coarse_solve(groups, nr, nc, out):
    shape = (W, 128)
    lane = iota(shape, 1)
    row_ok = wrap(iota(shape, 0) - 10 + lax.axis_index("px") * 4, nr) > 0
    plane_ok = (lane & 31) > 0
    low, high = lane < 32, lane >= 96
    n = len(groups)
    f = [g[0] for g in groups]
    m = [g[1] for g in groups]
    c = [g[2] for g in groups]
    col_ok = [wrap((lane >> 5) - 9 + 4 * k + lax.axis_index("py") * 2, nc) > 0 for k in range(n)]
    zero = jnp.zeros(shape, F32)

    def before(x, k):
        a = pltpu.roll(x[k], 32, 1)
        b = pltpu.roll(x[k - 1], 32, 1) if k else zero
        return jnp.where(low, b, a)

    def after(x, k):
        a = pltpu.roll(x[k], 96, 1)
        b = pltpu.roll(x[k + 1], 96, 1) if k + 1 < n else zero
        return jnp.where(high, b, a)

    sx = [jnp.where(row_ok, a + up(a), 0.0) for a in m]
    sy = [jnp.where(col_ok[k], a + before(m, k), 0.0) for k, a in enumerate(m)]
    sz = [jnp.where(plane_ok, a + left(a), 0.0) for a in m]
    v = [a * b for a, b in zip(c, f)]
    for _ in range(7):
        wy = [a * b for a, b in zip(sy, v)]
        new = []
        for k in range(n):
            x = v[k]
            total = f[k] + sx[k] * up(x) + down(sx[k] * x)
            total = total + sy[k] * before(v, k) + after(wy, k)
            total = total + sz[k] * left(x) + right(sz[k] * x)
            new.append(0.2 * x + c[k] * total)
        v = new
    for k in range(n):
        out[k] = v[k]


def ascent_kernel(levels, own, near0, near1, far0, far1, *refs):
    fields = [refs[6 * k : 6 * k + 6] for k in range(3)]
    result = refs[18]
    e3, p2, a2, b2, p1, q1, a1, b1, p0, q0, a0 = refs[19:]
    lv0, lv1, lv2 = levels
    position, count = lax.axis_index("py"), lax.axis_size("py")

    def outer(pair, step):
        prev, nxt = chooser("py", step)(pair[0][...], pair[1][...])
        turn = lambda t: pltpu.roll(t, 64, 2)
        prev = jnp.where(position < step, turn(prev), prev)
        return prev, jnp.where(position >= count - step, turn(nxt), nxt)

    before, after = outer((near0, near1), 2)
    first, last = outer((far0, far1), 4)
    coarse_solve([first, before, own[...], after, last], lv2.nrows // 2, lv2.ncols // 2, e3)

    p2[...] = jnp.zeros(p2.shape, F32)
    two = p2.reshape(8 * W, 128)
    for q in range(-2, 4):
        group, g = (q + 9) // 4, (q + 9) % 4
        spread = select_matrix((128, 128), lambda r, c: ((c >> 1) + 32 * g == r) & (c < 64))
        x = dot(e3[group, 8:16], spread)
        two[pl.ds((2 * q) % W, 8, stride=W)] = x
        two[pl.ds((2 * q + 1) % W, 8, stride=W)] = x
    v, rhs, sx, sy, sz, coef = fields[2]

    value2 = lambda i: v[i] + p2[i // 2 - 2]
    sweep(5, 19, value2, writer(b2), rhs, sx, sy, sz, coef)
    sweep(6, 18, reader(b2), writer(a2), rhs, sx, sy, sz, coef)

    for k in range(12):
        x = a2[k + 6]
        for s in range(2):
            p1[k, pl.ds(s, 8, stride=2)] = x[0:8]
            p1[k, pl.ds(16 + s, 4, stride=2)] = x[20:24]
    q1[...] = dot(p1[...].reshape(12 * W, 128), spread_planes(128, 0, 64)).reshape(12, W, 128)
    v1, rhs1, sx1, sy1, sz1, coef1 = fields[1]

    value1 = lambda i: v1[i] + q1[i // 2 - 1]
    sweep(4, 24, value1, writer(b1), rhs1, sx1, sy1, sz1, coef1)
    sweep(5, 23, reader(b1), writer(a1), rhs1, sx1, sy1, sz1, coef1)

    for k in range(18):
        x = a1[k + 5]
        for s in range(2):
            p0[k, pl.ds(s, 8, stride=2)] = x[0:8]
            p0[k, pl.ds(16 + s, 2, stride=2)] = x[8:10]
            p0[k, pl.ds(20 + s, 2, stride=2)] = x[22:24]
    q0[...] = dot(p0[...].reshape(18 * W, 128), spread_planes(256)).reshape(18, W, 256)
    v0, rhs0, sx0, sy0, sz0, coef0 = fields[0]

    value0 = lambda i: v0[i] + q0[i // 2 - 1]
    sweep(3, 37, value0, writer(a0), rhs0, sx0, sy0, sz0, coef0)

    def final(i, x):
        result[i - 4] = x[0:16]

    sweep(4, 36, reader(a0), final, rhs0, sx0, sy0, sz0, coef0)


VMEM = pl.BlockSpec(memory_space=pltpu.VMEM)
LIMIT = 14 << 20


def descend(kernel, lv, inputs, packed, scratch):
    block = jax.ShapeDtypeStruct((lv.total, W, lv.lanes), F32)
    outs = pl.pallas_call(
        lambda *refs: kernel(lv, *refs),
        out_shape=[jax.ShapeDtypeStruct(packed, F32)] + [block] * 6,
        in_specs=[VMEM] * len(inputs),
        out_specs=[VMEM] * 7,
        scratch_shapes=[pltpu.VMEM(block.shape, F32)] * 3 + [pltpu.VMEM(s, F32) for s in scratch],
        compiler_params=pltpu.CompilerParams(vmem_limit_bytes=LIMIT),
        name="descent",
    )(*inputs)
    return outs[0], outs[1:]


def is_odd(axis, step):
    return (lax.axis_index(axis) // step) % 2 == 1


def swap_partners(n, step, parity):
    partner = list(range(n))
    for i in range(n - step):
        if (i // step) % 2 == parity:
            partner[i], partner[i + step] = i + step, i
    alone = [i for i in range(n) if partner[i] == i]
    for group in (alone[:step], alone[step:]):
        for i, j in zip(group, reversed(group)):
            partner[i] = j
    return partner


def exchange(to_prev, to_next, odd, axis, step=1):
    n, other = lax.axis_size(axis), "py" if axis == "px" else "px"
    got = []
    for parity in range(2):
        partner = swap_partners(n, step, parity)
        pairs = []
        for i in range(n):
            for j in range(lax.axis_size(other)):
                a, b = (i, j), (partner[i], j if partner[i] != i else j ^ 1)
                if axis == "py":
                    a, b = a[::-1], b[::-1]
                pairs.append(tuple(p * lax.axis_size("py") + q for p, q in (a, b)))
        out = to_next if to_prev is to_next else jnp.where(odd == (parity == 0), to_prev, to_next)
        got.append(lax.ppermute(out, ("px", "py"), pairs))
    return got


def pick(got, odd):
    return jnp.where(odd, got[0], got[1]), jnp.where(odd, got[1], got[0])


def per_device(source, density):
    npx, npy = lax.axis_size("px"), lax.axis_size("py")
    lv0 = Level(32, 4, 16, 4, 256, 256, 32 * npx, 16 * npy)
    lv1 = Level(16, 6, 8, 8, 128, 128, 16 * npx, 8 * npy)
    lv2 = Level(8, 8, 4, 8, 128, 64, 8 * npx, 4 * npy)

    x, step_rows = lax.axis_index("px"), 2
    flags = (
        is_odd("px", 1), is_odd("py", 1), is_odd("px", step_rows),
        x < step_rows, x >= npx - step_rows,
    )
    source, density, (odd_x, odd_y, odd_2, first_x, last_x) = lax.optimization_barrier(
        (source, density, flags)
    )

    h = lv0.halo
    rows = exchange(
        jnp.concatenate([source[:h], density[:h]], 0),
        jnp.concatenate([source[-h:], density[-h:]], 0), odd_x, "px",
    )
    lo, hi = pick(rows, odd_x)
    to_right = lambda s, d: jnp.concatenate([d[:, 12:16], s[:, 12:16]], 1)
    to_left = lambda s, d: jnp.concatenate([s[:, 0:4], d[:, 0:4]], 1)
    sides = exchange(to_left(source, density), to_right(source, density), odd_y, "py")
    row_source = jnp.concatenate([lo[:h], hi[:h]], 0)
    row_density = jnp.concatenate([lo[h:], hi[h:]], 0)
    corners = exchange(
        to_left(row_source, row_density), to_right(row_source, row_density), odd_y, "py"
    )
    one, saved0 = descend(
        level0_kernel, lv0, (source, density, *rows, *sides, *corners),
        (16, W, 128), [(16, W, 256), (16 * W, 128)],
    )

    h = lv1.halo
    rows = exchange(one[:h], one[-h:], odd_x, "px")
    lo, hi = pick(rows, odd_x)
    wide = lambda a: jnp.concatenate([lo[:, a : a + 8], one[:, a : a + 8], hi[:, a : a + 8]], 0)
    sides = exchange(wide(8), wide(0), odd_y, "py")
    two, saved1 = descend(
        level1_kernel, lv1, (one, *rows, *sides), (8, 16, 128), [(8, W, 128), (8 * W, 128)],
    )

    rows = exchange(two, two, odd_x, "px")
    lo, hi = pick(rows, odd_x)
    wide = lambda a: jnp.concatenate([lo[:, a : a + 8], two[:, a : a + 8], hi[:, a : a + 8]], 0)
    sides = exchange(wide(8), wide(0), odd_y, "py")
    three, saved2 = descend(
        level2_kernel, lv2, (two, *rows, *sides), (3, 8, 128), [(8, W, 128), (16, W, 128)],
    )

    lo, hi = pick(exchange(three, three, odd_2, "px", step_rows), odd_2)
    turn = lambda t: jnp.concatenate([t[:, 4:], t[:, :4]], 1)
    lo, hi = jnp.where(first_x, turn(lo), lo), jnp.where(last_x, turn(hi), hi)
    wide = jnp.concatenate([lo, three, hi], 1)
    groups = (wide, *exchange(wide, wide, None, "py", 2), *exchange(wide, wide, None, "py", 4))
    inputs = (*groups, *saved0, *saved1, *saved2)
    shapes = [(5, W, 128), (8, W, 128), (24, W, 128), (24, W, 128), (12, W, 128), (12, W, 128),
              (28, W, 128), (28, W, 128), (18, W, 128), (18, W, 256), (40, W, 256)]
    return pl.pallas_call(
        lambda *refs: ascent_kernel((lv0, lv1, lv2), *refs),
        out_shape=jax.ShapeDtypeStruct(source.shape, F32),
        in_specs=[VMEM] * len(inputs),
        out_specs=VMEM,
        scratch_shapes=[pltpu.VMEM(s, F32) for s in shapes],
        compiler_params=pltpu.CompilerParams(vmem_limit_bytes=LIMIT),
        name="ascent",
    )(*inputs)


def solution(mesh):
    spec = P("px", "py", None)
    return jax.shard_map(
        per_device, mesh=mesh, in_specs=(spec, spec), out_specs=spec, check_vma=False
    )
```

```python
import jax
import jax.numpy as jnp
from jax import lax
from jax.experimental import pallas as pl
from jax.experimental.pallas import tpu as pltpu
from jax.sharding import PartitionSpec as P

F32 = jnp.float32
W = 24
BF16 = jnp.bfloat16
UNROLL = 4


def iota(shape, dim):
    return lax.broadcasted_iota(jnp.int32, shape, dim)


def up(x):
    return pltpu.roll(x, 1, 0)


def down(x):
    return pltpu.roll(x, x.shape[0] - 1, 0)


def left(x):
    return pltpu.roll(x, 1, 1)


def right(x):
    return pltpu.roll(x, x.shape[1] - 1, 1)


def dot(a, b):
    high = a.astype(BF16)
    rest = a - high.astype(F32)
    mid = rest.astype(BF16)
    low = (rest - mid.astype(F32)).astype(BF16)
    return sum(jnp.dot(x, b, preferred_element_type=F32) for x in (high, mid, low))


def select_matrix(shape, where):
    return jnp.where(where(iota(shape, 0), iota(shape, 1)), 1.0, 0.0).astype(BF16)


def wrap(x, n):
    return jnp.where(x < 0, x + n, jnp.where(x >= n, x - n, x))


class Level:
    def __init__(self, rows, halo, cols, right_cols, lanes, planes, nrows, ncols):
        self.rows, self.halo, self.cols, self.right_cols = rows, halo, cols, right_cols
        self.lanes, self.planes, self.nrows, self.ncols = lanes, planes, nrows, ncols
        self.total = rows + 2 * halo

    def masks(self):
        shape = (W, self.lanes)
        col = iota(shape, 0)
        col = jnp.where(col < self.cols + self.right_cols, col, col - W)
        col = wrap(col + lax.axis_index("py") * self.cols, self.ncols)
        lane = iota(shape, 1)
        edge = lambda hit: jnp.where(hit, 2.0, 0.0)
        extra = edge(col == 0) + edge(col == self.ncols - 1)
        extra = extra + edge(lane == 0) + edge(lane == self.planes - 1)
        return lane < self.planes, col > 0, (lane > 0) & (lane < self.planes), extra

    def global_row(self, i):
        return wrap(lax.axis_index("px") * self.rows - self.halo + i, self.nrows)


def prepare(level, mob, rhs, sx, sy, sz, coef, diag, out):
    inside, inner_col, inner_plane, extra = level.masks()

    def face(i, a, b):
        return (a + b) * jnp.where(level.global_row(i) == 0, 0.0, 1.0)

    def step(i, carry):
        m, wx = carry
        below = mob[i + 1]
        g = level.global_row(i)
        next_wx = face(i + 1, m, below)
        wy = jnp.where(inner_col, m + up(m), 0.0)
        wz = jnp.where(inner_plane, m + left(m), 0.0)
        sx[i + 1] = next_wx
        sy[i] = wy
        sz[i] = wz
        ends = jnp.where((g == 0) | (g == level.nrows - 1), 2.0, 0.0)
        d = (wx + next_wx) + (wy + down(wy)) + (wz + right(wz)) + (extra + ends) * m
        c = 0.8 / d
        if level.planes < level.lanes:
            c = jnp.where(inside, c, 0.0)
        coef[i] = c
        diag[i] = d
        out[i] = c * rhs[i]
        return below, next_wx

    first = face(1, mob[0], mob[1])
    sx[1] = first
    lax.fori_loop(1, level.total - 1, step, (mob[1], first), unroll=UNROLL if level.planes < 128 else 2 * UNROLL)


def walk(lo, hi, load, emit, sx, sy, sz):
    def step(i, carry):
        above, c, wx = carry
        below, next_wx = load(i + 1), sx[i + 1]
        wy, wz = sy[i], sz[i]
        total = (wx * above + next_wx * below) + (wy * up(c) + down(wy * c))
        total = total + (wz * left(c) + right(wz * c))
        emit(i, c, total)
        return c, below, next_wx

    unroll = UNROLL if hi - lo == 38 else 2 * UNROLL
    lax.fori_loop(lo, hi, step, (load(lo - 1), load(lo), sx[lo]), unroll=unroll)


def sweep(lo, hi, load, store, rhs, sx, sy, sz, coef):
    def emit(i, c, total):
        store(i, 0.2 * c + coef[i] * (rhs[i] + total))

    walk(lo, hi, load, emit, sx, sy, sz)


def reader(ref):
    return lambda i: ref[i]


def writer(ref):
    def store(i, x):
        ref[i] = x

    return store


def paired_residual(pairs, lo, cols, v, out, rhs, sx, sy, sz, diag):
    def step(k, carry):
        above, c, wx = carry
        done = []
        for j in range(2):
            i = lo + 2 * k + j
            below, next_wx = v[i + 1], sx[i + 1]
            wy, wz = sy[i], sz[i]
            total = (wx * above + next_wx * below) + (wy * up(c) + down(wy * c))
            total = total + (wz * left(c) + right(wz * c))
            done.append((rhs[i] - diag[i] * c + total)[0:cols])
            above, c, wx = c, below, next_wx
        out[k] = done[0] + done[1]
        return above, c, wx

    lax.fori_loop(0, pairs, step, (v[lo - 1], v[lo], sx[lo]), unroll=UNROLL)


def pair_planes(lanes_in, offset=0, lanes_out=128):
    return select_matrix((lanes_in, lanes_out), lambda r, c: (r >> 1) + offset == c)


def spread_planes(lanes_out, offset=0, planes=128):
    return select_matrix((128, lanes_out), lambda r, c: ((c >> 1) + offset == r) & ((c >> 1) < planes))


def chooser(axis, step=1):
    odd = is_odd(axis, step)
    return lambda a, b: (jnp.where(odd, a, b), jnp.where(odd, b, a))


def halo_readers(rows0, rows1):
    choose = chooser("px")
    lo = lambda i: choose(rows0[i], rows1[i])[0]
    hi = lambda i: choose(rows0[i], rows1[i])[1]
    return lo, hi, chooser("py")


def level0_kernel(lv, src, dens, rows0, rows1, sides0, sides1, corners0, corners1, packed, v, rhs, sx, sy, sz, coef,
                  mob, first, diag, pair, low):
    h = lv.halo
    tile = iota((8, lv.lanes), 0)
    lo, hi, choose = halo_readers(rows0, rows1)

    def load(i, s, d, a, b):
        rhs[i, 0:16] = 2.0 * s
        mob[i, 0:16] = 1.0 / d
        rhs[i, 16:24] = 2.0 * jnp.where(tile < 4, a, b)
        mob[i, 16:24] = 1.0 / pltpu.roll(jnp.where(tile < 4, b, a), 4, 0)

    for i in range(h):
        left_side, right_side = choose(corners0[i], corners1[i])
        load(i, lo(i), lo(h + i), right_side, left_side)
        left_side, right_side = choose(corners0[h + i], corners1[h + i])
        load(lv.total - h + i, hi(i), hi(h + i), right_side, left_side)

    def body(i, carry):
        left_side, right_side = choose(sides0[i], sides1[i])
        load(h + i, src[i], dens[i], right_side, left_side)
        return carry

    lax.fori_loop(0, lv.rows, body, 0, unroll=UNROLL)
    zero = jnp.zeros((W, lv.lanes), F32)
    for ref in (first, v):
        ref[0] = zero
        ref[lv.total - 1] = zero
    prepare(lv, mob, rhs, sx, sy, sz, coef, diag, first)
    sweep(1, lv.total - 1, reader(first), writer(v), rhs, sx, sy, sz, coef)
    half = lv.rows // 2
    z = pair_planes(lv.lanes)
    paired_residual(half, h, 16, v, pair.at[:, 0:16], rhs, sx, sy, sz, diag)

    low[0 : half * 16] = 0.5 * dot(pair[:, 0:16].reshape(half * 16, lv.lanes), z)
    fine = low[pl.ds(0, half * 8, stride=2)] + low[pl.ds(1, half * 8, stride=2)]

    def mobs(k, carry):
        pair[k] = mob[h + 2 * k] + mob[h + 2 * k + 1]
        return carry

    lax.fori_loop(0, half, mobs, 0, unroll=UNROLL)
    low[...] = 0.125 * dot(pair[...].reshape(half * W, lv.lanes), z)
    at = iota((8, 128), 0)
    beside = jnp.zeros((4, 128), F32)
    for k in range(half):
        f = fine[8 * k : 8 * k + 8]
        m = low[pl.ds(k * W, 8, stride=2)] + low[pl.ds(k * W + 1, 8, stride=2)]
        e = low[pl.ds(k * W + 16, 4, stride=2)] + low[pl.ds(k * W + 17, 4, stride=2)]
        e = pltpu.roll(jnp.concatenate([e, beside], 0), 2, 0)
        shifted = pltpu.roll(m, 2, 0)
        packed[k, 0:8] = jnp.where(at < 4, pltpu.roll(f, 4, 0), shifted)
        packed[k, 8:16] = jnp.where(at < 4, f, shifted)
        packed[k, 16:24] = jnp.where((at < 2) | (at >= 6), m, e)


def level1_kernel(lv, own, rows0, rows1, sides0, sides1, packed, v, rhs, sx, sy, sz, coef,
                  mob, first, diag, pair, low):
    h = lv.halo

    at = iota((8, lv.lanes), 0)
    lo, hi, choose = halo_readers(rows0, rows1)

    def load(i, block):
        t0, t1, t2 = block[0:8], block[8:16], block[16:24]
        b, a = choose(sides0[i], sides1[i])
        rhs[i, 0:8] = jnp.where(at < 4, t1, pltpu.roll(t0, 4, 0))
        rhs[i, 8:16] = a
        rhs[i, 16:24] = pltpu.roll(b, 4, 0)
        mob[i, 0:8] = jnp.where((at < 2) | (at >= 6), t2, pltpu.roll(t0, 6, 0))
        far = jnp.where(at < 6, pltpu.roll(a, 6, 0), 1.0)
        mob[i, 8:16] = jnp.where(at < 2, pltpu.roll(t2, 6, 0), far)
        far = jnp.where(at < 2, 1.0, pltpu.roll(b, 6, 0))
        mob[i, 16:24] = jnp.where(at < 6, far, pltpu.roll(t2, 2, 0))

    for i in range(h):
        load(i, lo(i))
        load(lv.total - h + i, hi(i))

    def body(i, carry):
        load(h + i, own[i])
        return carry

    lax.fori_loop(0, lv.rows, body, 0, unroll=UNROLL)
    zero = jnp.zeros((W, lv.lanes), F32)
    for ref in (first, v):
        ref[0] = zero
        ref[lv.total - 1] = zero
    prepare(lv, mob, rhs, sx, sy, sz, coef, diag, first)
    sweep(1, lv.total - 1, reader(first), writer(v), rhs, sx, sy, sz, coef)
    half = lv.rows // 2
    paired_residual(half, h, W, v, pair, rhs, sx, sy, sz, diag)
    x = 0.5 * dot(pair[...].reshape(half * W, lv.lanes), pair_planes(lv.lanes))

    def mobs(k, carry):
        pair[k] = mob[h + 2 * k] + mob[h + 2 * k + 1]
        return carry

    lax.fori_loop(0, half, mobs, 0)
    low[...] = x + 0.125 * dot(pair[...].reshape(half * W, lv.lanes), pair_planes(lv.lanes, 64))
    for k in range(half):
        a = k * W
        y = low[pl.ds(a, 8, stride=2)] + low[pl.ds(a + 1, 8, stride=2)]
        packed[k, 8:16] = y
        packed[k, 4:8] = y[0:4]
        packed[k, 0:4] = low[pl.ds(a + 16, 4, stride=2)] + low[pl.ds(a + 17, 4, stride=2)]


def level2_kernel(lv, own, rows0, rows1, sides0, sides1, packed, v, rhs, sx, sy, sz, coef,
                  mob, first, diag, pair, wide):
    h = lv.halo
    tile = iota((8, 128), 0)
    lane = iota((8, 128), 1) < lv.planes
    lo, hi, choose = halo_readers(rows0, rows1)

    def load(i, block):
        l, r = choose(sides0[i], sides1[i])
        r = pltpu.roll(r, 4, 0)
        parts = (jnp.where(tile < 4, block, r), r, l)
        for k, part in enumerate(parts):
            rhs[i, 8 * k : 8 * k + 8] = jnp.where(lane, part, 0.0)
            mob[i, 8 * k : 8 * k + 8] = jnp.where(lane, pltpu.roll(part, 64, 1), 1.0)

    for i in range(h):
        load(i, lo(i)[8:16])
        load(h + i, own[i, 8:16])
        load(2 * h + i, hi(i)[8:16])
    zero = jnp.zeros((W, lv.lanes), F32)
    for ref in (first, v):
        ref[0] = zero
        ref[lv.total - 1] = zero
    prepare(lv, mob, rhs, sx, sy, sz, coef, diag, first)
    sweep(1, lv.total - 1, reader(first), writer(v), rhs, sx, sy, sz, coef)
    paired_residual(8, 4, W, v, pair, rhs, sx, sy, sz, diag)
    for k in range(12):
        wide[k] = mob[2 * k] + mob[2 * k + 1]
    for k in range(12, 16):
        wide[k] = zero

    def column(ref, n, q):
        two = ref.reshape(n * W, 128)
        return two[pl.ds((2 * q) % W, n, stride=W)] + two[pl.ds((2 * q + 1) % W, n, stride=W)]

    f = jnp.zeros((8, 128), F32)
    m = jnp.zeros((16, 128), F32)
    for g in range(4):
        place = select_matrix((128, 128), lambda r, c: ((r >> 1) + 32 * g == c) & (r < 64))
        f = f + dot(column(pair, 8, g - 1), place)
        m = m + dot(column(wide, 16, g - 1), place)
    f, m = 0.5 * f, 0.125 * m
    p0 = select_matrix((128, 128), lambda r, c: ((r >> 1) + 96 == c) & (r < 64))
    p3 = select_matrix((128, 128), lambda r, c: ((r >> 1) == c) & (r < 64))
    beside = 0.125 * (dot(column(wide, 16, -2), p0) + dot(column(wide, 16, 3), p3))
    lanes = iota((16, 128), 1)
    nr, nc = lv.nrows // 2, lv.ncols // 2
    row = wrap(iota((16, 128), 0) - 4 + lax.axis_index("px") * 4, nr)
    col = wrap((lanes >> 5) - 1 + lax.axis_index("py") * 2, nc)
    prev = jnp.where(lanes < 32, pltpu.roll(beside, 32, 1), pltpu.roll(m, 32, 1))
    nxt = jnp.where(lanes >= 96, pltpu.roll(beside, 96, 1), pltpu.roll(m, 96, 1))
    d = 6.0 * m + jnp.where(row == 0, m, up(m)) + jnp.where(row == nr - 1, m, down(m))
    d = d + jnp.where(col == 0, m, prev) + jnp.where(col == nc - 1, m, nxt)
    plane = lanes & 31
    d = d + jnp.where(plane == 0, m, left(m)) + jnp.where(plane == 31, m, right(m))
    packed[0] = f
    packed[1] = m[2:10]
    packed[2] = (0.8 / d)[2:10]


def coarse_solve(groups, nr, nc, out):
    shape = (W, 128)
    lane = iota(shape, 1)
    row_ok = wrap(iota(shape, 0) - 10 + lax.axis_index("px") * 4, nr) > 0
    plane_ok = (lane & 31) > 0
    low, high = lane < 32, lane >= 96
    n = len(groups)
    f = [g[0] for g in groups]
    m = [g[1] for g in groups]
    c = [g[2] for g in groups]
    col_ok = [wrap((lane >> 5) - 9 + 4 * k + lax.axis_index("py") * 2, nc) > 0 for k in range(n)]
    zero = jnp.zeros(shape, F32)

    def before(x, k):
        a = pltpu.roll(x[k], 32, 1)
        b = pltpu.roll(x[k - 1], 32, 1) if k else zero
        return jnp.where(low, b, a)

    def after(x, k):
        a = pltpu.roll(x[k], 96, 1)
        b = pltpu.roll(x[k + 1], 96, 1) if k + 1 < n else zero
        return jnp.where(high, b, a)

    sx = [jnp.where(row_ok, a + up(a), 0.0) for a in m]
    sy = [jnp.where(col_ok[k], a + before(m, k), 0.0) for k, a in enumerate(m)]
    sz = [jnp.where(plane_ok, a + left(a), 0.0) for a in m]
    v = [a * b for a, b in zip(c, f)]
    for _ in range(7):
        wy = [a * b for a, b in zip(sy, v)]
        new = []
        for k in range(n):
            x = v[k]
            total = f[k] + sx[k] * up(x) + down(sx[k] * x)
            total = total + sy[k] * before(v, k) + after(wy, k)
            total = total + sz[k] * left(x) + right(sz[k] * x)
            new.append(0.2 * x + c[k] * total)
        v = new
    for k in range(n):
        out[k] = v[k]


def ascent_kernel(levels, own, near0, near1, far0, far1, *refs):
    fields = [refs[6 * k : 6 * k + 6] for k in range(3)]
    result = refs[18]
    e3, p2, a2, b2, p1, q1, a1, b1, p0, q0, a0 = refs[19:]
    lv0, lv1, lv2 = levels
    position, count = lax.axis_index("py"), lax.axis_size("py")

    def outer(pair, step):
        prev, nxt = chooser("py", step)(pair[0][...], pair[1][...])
        turn = lambda t: pltpu.roll(t, 64, 2)
        prev = jnp.where(position < step, turn(prev), prev)
        return prev, jnp.where(position >= count - step, turn(nxt), nxt)

    before, after = outer((near0, near1), 2)
    first, last = outer((far0, far1), 4)
    coarse_solve([first, before, own[...], after, last], lv2.nrows // 2, lv2.ncols // 2, e3)

    p2[...] = jnp.zeros(p2.shape, F32)
    two = p2.reshape(8 * W, 128)
    for q in range(-2, 4):
        group, g = (q + 9) // 4, (q + 9) % 4
        spread = select_matrix((128, 128), lambda r, c: ((c >> 1) + 32 * g == r) & (c < 64))
        x = dot(e3[group, 8:16], spread)
        two[pl.ds((2 * q) % W, 8, stride=W)] = x
        two[pl.ds((2 * q + 1) % W, 8, stride=W)] = x
    v, rhs, sx, sy, sz, coef = fields[2]

    value2 = lambda i: v[i] + p2[i // 2 - 2]
    sweep(5, 19, value2, writer(b2), rhs, sx, sy, sz, coef)
    sweep(6, 18, reader(b2), writer(a2), rhs, sx, sy, sz, coef)

    for k in range(12):
        x = a2[k + 6]
        for s in range(2):
            p1[k, pl.ds(s, 8, stride=2)] = x[0:8]
            p1[k, pl.ds(16 + s, 4, stride=2)] = x[20:24]
    q1[...] = dot(p1[...].reshape(12 * W, 128), spread_planes(128, 0, 64)).reshape(12, W, 128)
    v1, rhs1, sx1, sy1, sz1, coef1 = fields[1]

    value1 = lambda i: v1[i] + q1[i // 2 - 1]
    sweep(4, 24, value1, writer(b1), rhs1, sx1, sy1, sz1, coef1)
    sweep(5, 23, reader(b1), writer(a1), rhs1, sx1, sy1, sz1, coef1)

    for k in range(18):
        x = a1[k + 5]
        for s in range(2):
            p0[k, pl.ds(s, 8, stride=2)] = x[0:8]
            p0[k, pl.ds(16 + s, 2, stride=2)] = x[8:10]
            p0[k, pl.ds(20 + s, 2, stride=2)] = x[22:24]
    q0[...] = dot(p0[...].reshape(18 * W, 128), spread_planes(256)).reshape(18, W, 256)
    v0, rhs0, sx0, sy0, sz0, coef0 = fields[0]

    value0 = lambda i: v0[i] + q0[i // 2 - 1]
    sweep(3, 37, value0, writer(a0), rhs0, sx0, sy0, sz0, coef0)

    def final(i, x):
        result[i - 4] = x[0:16]

    sweep(4, 36, reader(a0), final, rhs0, sx0, sy0, sz0, coef0)


VMEM = pl.BlockSpec(memory_space=pltpu.VMEM)
LIMIT = 14 << 20


def descend(kernel, lv, inputs, packed, scratch):
    block = jax.ShapeDtypeStruct((lv.total, W, lv.lanes), F32)
    outs = pl.pallas_call(
        lambda *refs: kernel(lv, *refs),
        out_shape=[jax.ShapeDtypeStruct(packed, F32)] + [block] * 6,
        in_specs=[VMEM] * len(inputs),
        out_specs=[VMEM] * 7,
        scratch_shapes=[pltpu.VMEM(block.shape, F32)] * 3 + [pltpu.VMEM(s, F32) for s in scratch],
        compiler_params=pltpu.CompilerParams(vmem_limit_bytes=LIMIT),
        name="descent",
    )(*inputs)
    return outs[0], outs[1:]


def is_odd(axis, step):
    return (lax.axis_index(axis) & step) != 0


def swap_partners(n, step, parity):
    partner = list(range(n))
    for i in range(n - step):
        if (i // step) % 2 == parity:
            partner[i], partner[i + step] = i + step, i
    alone = [i for i in range(n) if partner[i] == i]
    for group in (alone[:step], alone[step:]):
        for i, j in zip(group, reversed(group)):
            partner[i] = j
    return partner


def exchange(to_prev, to_next, odd, axis, step=1):
    n, other = lax.axis_size(axis), "py" if axis == "px" else "px"
    got = []
    for parity in range(2):
        partner = swap_partners(n, step, parity)
        pairs = []
        for i in range(n):
            for j in range(lax.axis_size(other)):
                a, b = (i, j), (partner[i], j if partner[i] != i else j ^ 1)
                if axis == "py":
                    a, b = a[::-1], b[::-1]
                pairs.append(tuple(p * lax.axis_size("py") + q for p, q in (a, b)))
        if to_prev is None:
            out = to_next[parity]
        elif to_prev is to_next:
            out = to_next
        else:
            out = jnp.where(odd == (parity == 0), to_prev, to_next)
        got.append(lax.ppermute(out, ("px", "py"), pairs))
    return got


def pick(got, odd):
    return jnp.where(odd, got[0], got[1]), jnp.where(odd, got[1], got[0])


def per_device(source, density):
    npx, npy = lax.axis_size("px"), lax.axis_size("py")
    lv0 = Level(32, 4, 16, 4, 256, 256, 32 * npx, 16 * npy)
    lv1 = Level(16, 6, 8, 8, 128, 128, 16 * npx, 8 * npy)
    lv2 = Level(8, 8, 4, 8, 128, 64, 8 * npx, 4 * npy)

    x, step_rows = lax.axis_index("px"), 2
    flags = (
        is_odd("px", 1), is_odd("py", 1), is_odd("px", step_rows),
        x < step_rows, x >= npx - step_rows,
        ((1 - (x & 1)) * (lv0.rows - lv0.halo), (x & 1) * (lv0.rows - lv0.halo)),
    )
    source, density, (odd_x, odd_y, odd_2, first_x, last_x, starts) = lax.optimization_barrier(
        (source, density, flags)
    )

    h = lv0.halo
    edge_rows = [
        jnp.concatenate([lax.dynamic_slice_in_dim(a, at, h, 0) for a in (source, density)], 0)
        for at in starts
    ]
    rows = exchange(None, edge_rows, odd_x, "px")
    lo, hi = pick(rows, odd_x)
    to_right = lambda s, d: jnp.concatenate([d[:, 12:16], s[:, 12:16]], 1)
    to_left = lambda s, d: jnp.concatenate([s[:, 0:4], d[:, 0:4]], 1)
    sides = exchange(to_left(source, density), to_right(source, density), odd_y, "py")
    row_source = jnp.concatenate([lo[:h], hi[:h]], 0)
    row_density = jnp.concatenate([lo[h:], hi[h:]], 0)
    corners = exchange(
        to_left(row_source, row_density), to_right(row_source, row_density), odd_y, "py"
    )
    one, saved0 = descend(
        level0_kernel, lv0, (source, density, *rows, *sides, *corners),
        (16, W, 128), [(16, W, 256), (16 * W, 128)],
    )

    h = lv1.halo
    rows = exchange(one[:h], one[-h:], odd_x, "px")
    lo, hi = pick(rows, odd_x)
    wide = lambda a: jnp.concatenate([lo[:, a : a + 8], one[:, a : a + 8], hi[:, a : a + 8]], 0)
    sides = exchange(wide(8), wide(0), odd_y, "py")
    two, saved1 = descend(
        level1_kernel, lv1, (one, *rows, *sides), (8, 16, 128), [(8, W, 128), (8 * W, 128)],
    )

    rows = exchange(two, two, odd_x, "px")
    lo, hi = pick(rows, odd_x)
    wide = lambda a: jnp.concatenate([lo[:, a : a + 8], two[:, a : a + 8], hi[:, a : a + 8]], 0)
    sides = exchange(wide(8), wide(0), odd_y, "py")
    three, saved2 = descend(
        level2_kernel, lv2, (two, *rows, *sides), (3, 8, 128), [(8, W, 128), (16, W, 128)],
    )

    lo, hi = pick(exchange(three, three, odd_2, "px", step_rows), odd_2)
    turn = lambda t: jnp.concatenate([t[:, 4:], t[:, :4]], 1)
    lo, hi = jnp.where(first_x, turn(lo), lo), jnp.where(last_x, turn(hi), hi)
    wide = jnp.concatenate([lo, three, hi], 1)
    groups = (wide, *exchange(wide, wide, None, "py", 2), *exchange(wide, wide, None, "py", 4))
    inputs = (*groups, *saved0, *saved1, *saved2)
    shapes = [(5, W, 128), (8, W, 128), (24, W, 128), (24, W, 128), (12, W, 128), (12, W, 128),
              (28, W, 128), (28, W, 128), (18, W, 128), (18, W, 256), (40, W, 256)]
    return pl.pallas_call(
        lambda *refs: ascent_kernel((lv0, lv1, lv2), *refs),
        out_shape=jax.ShapeDtypeStruct(source.shape, F32),
        in_specs=[VMEM] * len(inputs),
        out_specs=VMEM,
        scratch_shapes=[pltpu.VMEM(s, F32) for s in shapes],
        compiler_params=pltpu.CompilerParams(vmem_limit_bytes=LIMIT),
        name="ascent",
    )(*inputs)


def solution(mesh):
    spec = P("px", "py", None)
    return jax.shard_map(
        per_device, mesh=mesh, in_specs=(spec, spec), out_specs=spec, check_vma=False
    )
```

```python
import jax
import jax.numpy as jnp
from jax import lax
from jax.experimental import pallas as pl
from jax.experimental.pallas import tpu as pltpu
from jax.sharding import PartitionSpec as P

F32 = jnp.float32
W = 24
BF16 = jnp.bfloat16
UNROLL = 4


def iota(shape, dim):
    return lax.broadcasted_iota(jnp.int32, shape, dim)


def up(x):
    return pltpu.roll(x, 1, 0)


def down(x):
    return pltpu.roll(x, x.shape[0] - 1, 0)


def left(x):
    return pltpu.roll(x, 1, 1)


def right(x):
    return pltpu.roll(x, x.shape[1] - 1, 1)


def dot(a, b):
    high = a.astype(BF16)
    rest = a - high.astype(F32)
    mid = rest.astype(BF16)
    low = (rest - mid.astype(F32)).astype(BF16)
    return sum(jnp.dot(x, b, preferred_element_type=F32) for x in (high, mid, low))


def select_matrix(shape, where):
    return jnp.where(where(iota(shape, 0), iota(shape, 1)), 1.0, 0.0).astype(BF16)


def wrap(x, n):
    return jnp.where(x < 0, x + n, jnp.where(x >= n, x - n, x))


class Level:
    def __init__(self, rows, halo, cols, right_cols, lanes, planes, nrows, ncols):
        self.rows, self.halo, self.cols, self.right_cols = rows, halo, cols, right_cols
        self.lanes, self.planes, self.nrows, self.ncols = lanes, planes, nrows, ncols
        self.total = rows + 2 * halo

    def masks(self):
        shape = (W, self.lanes)
        col = iota(shape, 0)
        col = jnp.where(col < self.cols + self.right_cols, col, col - W)
        col = wrap(col + lax.axis_index("py") * self.cols, self.ncols)
        lane = iota(shape, 1)
        edge = lambda hit: jnp.where(hit, 2.0, 0.0)
        extra = edge(col == 0) + edge(col == self.ncols - 1)
        extra = extra + edge(lane == 0) + edge(lane == self.planes - 1)
        return lane < self.planes, col > 0, (lane > 0) & (lane < self.planes), extra

    def global_row(self, i):
        return wrap(lax.axis_index("px") * self.rows - self.halo + i, self.nrows)


def prepare(level, mob, rhs, sx, sy, sz, coef, diag, out):
    inside, inner_col, inner_plane, extra = level.masks()

    def face(i, a, b):
        return (a + b) * jnp.where(level.global_row(i) == 0, 0.0, 1.0)

    def step(i, carry):
        m, wx = carry
        below = mob[i + 1]
        g = level.global_row(i)
        next_wx = face(i + 1, m, below)
        wy = jnp.where(inner_col, m + up(m), 0.0)
        wz = jnp.where(inner_plane, m + left(m), 0.0)
        sx[i + 1] = next_wx
        sy[i] = wy
        sz[i] = wz
        ends = jnp.where((g == 0) | (g == level.nrows - 1), 2.0, 0.0)
        d = (wx + next_wx) + (wy + down(wy)) + (wz + right(wz)) + (extra + ends) * m
        c = 0.8 / d
        if level.planes < level.lanes:
            c = jnp.where(inside, c, 0.0)
        coef[i] = c
        diag[i] = d
        out[i] = c * rhs[i]
        return below, next_wx

    first = face(1, mob[0], mob[1])
    sx[1] = first
    lax.fori_loop(1, level.total - 1, step, (mob[1], first), unroll=level.total - 2)


def walk(lo, hi, load, emit, sx, sy, sz):
    def step(i, carry):
        above, c, wx = carry
        below, next_wx = load(i + 1), sx[i + 1]
        wy, wz = sy[i], sz[i]
        total = (wx * above + next_wx * below) + (wy * up(c) + down(wy * c))
        total = total + (wz * left(c) + right(wz * c))
        emit(i, c, total)
        return c, below, next_wx

    unroll = hi - lo
    lax.fori_loop(lo, hi, step, (load(lo - 1), load(lo), sx[lo]), unroll=unroll)


def sweep(lo, hi, load, store, rhs, sx, sy, sz, coef):
    def emit(i, c, total):
        store(i, 0.2 * c + coef[i] * (rhs[i] + total))

    walk(lo, hi, load, emit, sx, sy, sz)


def reader(ref):
    return lambda i: ref[i]


def writer(ref):
    def store(i, x):
        ref[i] = x

    return store


def paired_residual(pairs, lo, cols, v, out, rhs, sx, sy, sz, diag):
    def step(k, carry):
        above, c, wx = carry
        done = []
        for j in range(2):
            i = lo + 2 * k + j
            below, next_wx = v[i + 1], sx[i + 1]
            wy, wz = sy[i], sz[i]
            total = (wx * above + next_wx * below) + (wy * up(c) + down(wy * c))
            total = total + (wz * left(c) + right(wz * c))
            done.append((rhs[i] - diag[i] * c + total)[0:cols])
            above, c, wx = c, below, next_wx
        out[k] = done[0] + done[1]
        return above, c, wx

    lax.fori_loop(0, pairs, step, (v[lo - 1], v[lo], sx[lo]), unroll=pairs)


def pair_planes(lanes_in, offset=0, lanes_out=128):
    return select_matrix((lanes_in, lanes_out), lambda r, c: (r >> 1) + offset == c)


def spread_planes(lanes_out, offset=0, planes=128):
    return select_matrix((128, lanes_out), lambda r, c: ((c >> 1) + offset == r) & ((c >> 1) < planes))


def chooser(axis, step=1):
    odd = is_odd(axis, step)
    return lambda a, b: (jnp.where(odd, a, b), jnp.where(odd, b, a))


def halo_readers(rows0, rows1):
    choose = chooser("px")
    lo = lambda i: choose(rows0[i], rows1[i])[0]
    hi = lambda i: choose(rows0[i], rows1[i])[1]
    return lo, hi, chooser("py")


def level0_kernel(lv, src, dens, rows0, rows1, sides0, sides1, corners0, corners1, packed, v, rhs, sx, sy, sz, coef,
                  mob, first, diag, pair, low):
    h = lv.halo
    tile = iota((8, lv.lanes), 0)
    lo, hi, choose = halo_readers(rows0, rows1)

    def load(i, s, d, a, b):
        rhs[i, 0:16] = 2.0 * s
        mob[i, 0:16] = 1.0 / d
        rhs[i, 16:24] = 2.0 * jnp.where(tile < 4, a, b)
        mob[i, 16:24] = 1.0 / pltpu.roll(jnp.where(tile < 4, b, a), 4, 0)

    for i in range(h):
        left_side, right_side = choose(corners0[i], corners1[i])
        load(i, lo(i), lo(h + i), right_side, left_side)
        left_side, right_side = choose(corners0[h + i], corners1[h + i])
        load(lv.total - h + i, hi(i), hi(h + i), right_side, left_side)

    def body(i, carry):
        left_side, right_side = choose(sides0[i], sides1[i])
        load(h + i, src[i], dens[i], right_side, left_side)
        return carry

    lax.fori_loop(0, lv.rows, body, 0, unroll=lv.rows)
    zero = jnp.zeros((W, lv.lanes), F32)
    for ref in (first, v):
        ref[0] = zero
        ref[lv.total - 1] = zero
    prepare(lv, mob, rhs, sx, sy, sz, coef, diag, first)
    sweep(1, lv.total - 1, reader(first), writer(v), rhs, sx, sy, sz, coef)
    half = lv.rows // 2
    z = pair_planes(lv.lanes)
    paired_residual(half, h, 16, v, pair.at[:, 0:16], rhs, sx, sy, sz, diag)

    low[0 : half * 16] = 0.5 * dot(pair[:, 0:16].reshape(half * 16, lv.lanes), z)
    fine = low[pl.ds(0, half * 8, stride=2)] + low[pl.ds(1, half * 8, stride=2)]

    def mobs(k, carry):
        pair[k] = mob[h + 2 * k] + mob[h + 2 * k + 1]
        return carry

    lax.fori_loop(0, half, mobs, 0, unroll=8)
    low[...] = 0.125 * dot(pair[...].reshape(half * W, lv.lanes), z)
    at = iota((8, 128), 0)
    beside = jnp.zeros((4, 128), F32)
    for k in range(half):
        f = fine[8 * k : 8 * k + 8]
        m = low[pl.ds(k * W, 8, stride=2)] + low[pl.ds(k * W + 1, 8, stride=2)]
        e = low[pl.ds(k * W + 16, 4, stride=2)] + low[pl.ds(k * W + 17, 4, stride=2)]
        e = pltpu.roll(jnp.concatenate([e, beside], 0), 2, 0)
        shifted = pltpu.roll(m, 2, 0)
        packed[k, 0:8] = jnp.where(at < 4, pltpu.roll(f, 4, 0), shifted)
        packed[k, 8:16] = jnp.where(at < 4, f, shifted)
        packed[k, 16:24] = jnp.where((at < 2) | (at >= 6), m, e)


def level1_kernel(lv, own, rows0, rows1, sides0, sides1, packed, v, rhs, sx, sy, sz, coef,
                  mob, first, diag, pair, low):
    h = lv.halo

    at = iota((8, lv.lanes), 0)
    lo, hi, choose = halo_readers(rows0, rows1)

    def load(i, block):
        t0, t1, t2 = block[0:8], block[8:16], block[16:24]
        b, a = choose(sides0[i], sides1[i])
        rhs[i, 0:8] = jnp.where(at < 4, t1, pltpu.roll(t0, 4, 0))
        rhs[i, 8:16] = a
        rhs[i, 16:24] = pltpu.roll(b, 4, 0)
        mob[i, 0:8] = jnp.where((at < 2) | (at >= 6), t2, pltpu.roll(t0, 6, 0))
        far = jnp.where(at < 6, pltpu.roll(a, 6, 0), 1.0)
        mob[i, 8:16] = jnp.where(at < 2, pltpu.roll(t2, 6, 0), far)
        far = jnp.where(at < 2, 1.0, pltpu.roll(b, 6, 0))
        mob[i, 16:24] = jnp.where(at < 6, far, pltpu.roll(t2, 2, 0))

    for i in range(h):
        load(i, lo(i))
        load(lv.total - h + i, hi(i))

    def body(i, carry):
        load(h + i, own[i])
        return carry

    lax.fori_loop(0, lv.rows, body, 0, unroll=lv.rows)
    zero = jnp.zeros((W, lv.lanes), F32)
    for ref in (first, v):
        ref[0] = zero
        ref[lv.total - 1] = zero
    prepare(lv, mob, rhs, sx, sy, sz, coef, diag, first)
    sweep(1, lv.total - 1, reader(first), writer(v), rhs, sx, sy, sz, coef)
    half = lv.rows // 2
    paired_residual(half, h, W, v, pair, rhs, sx, sy, sz, diag)
    x = 0.5 * dot(pair[...].reshape(half * W, lv.lanes), pair_planes(lv.lanes))

    def mobs(k, carry):
        pair[k] = mob[h + 2 * k] + mob[h + 2 * k + 1]
        return carry

    lax.fori_loop(0, half, mobs, 0, unroll=8)
    low[...] = x + 0.125 * dot(pair[...].reshape(half * W, lv.lanes), pair_planes(lv.lanes, 64))
    for k in range(half):
        a = k * W
        y = low[pl.ds(a, 8, stride=2)] + low[pl.ds(a + 1, 8, stride=2)]
        packed[k, 8:16] = y
        packed[k, 4:8] = y[0:4]
        packed[k, 0:4] = low[pl.ds(a + 16, 4, stride=2)] + low[pl.ds(a + 17, 4, stride=2)]


def level2_kernel(lv, own, rows0, rows1, sides0, sides1, packed, v, rhs, sx, sy, sz, coef,
                  mob, first, diag, pair, wide):
    h = lv.halo
    tile = iota((8, 128), 0)
    lane = iota((8, 128), 1) < lv.planes
    lo, hi, choose = halo_readers(rows0, rows1)

    def load(i, block):
        l, r = choose(sides0[i], sides1[i])
        r = pltpu.roll(r, 4, 0)
        parts = (jnp.where(tile < 4, block, r), r, l)
        for k, part in enumerate(parts):
            rhs[i, 8 * k : 8 * k + 8] = jnp.where(lane, part, 0.0)
            mob[i, 8 * k : 8 * k + 8] = jnp.where(lane, pltpu.roll(part, 64, 1), 1.0)

    for i in range(h):
        load(i, lo(i)[8:16])
        load(h + i, own[i, 8:16])
        load(2 * h + i, hi(i)[8:16])
    zero = jnp.zeros((W, lv.lanes), F32)
    for ref in (first, v):
        ref[0] = zero
        ref[lv.total - 1] = zero
    prepare(lv, mob, rhs, sx, sy, sz, coef, diag, first)
    sweep(1, lv.total - 1, reader(first), writer(v), rhs, sx, sy, sz, coef)
    paired_residual(8, 4, W, v, pair, rhs, sx, sy, sz, diag)
    for k in range(12):
        wide[k] = mob[2 * k] + mob[2 * k + 1]
    for k in range(12, 16):
        wide[k] = zero

    def column(ref, n, q):
        two = ref.reshape(n * W, 128)
        return two[pl.ds((2 * q) % W, n, stride=W)] + two[pl.ds((2 * q + 1) % W, n, stride=W)]

    f = jnp.zeros((8, 128), F32)
    m = jnp.zeros((16, 128), F32)
    for g in range(4):
        place = select_matrix((128, 128), lambda r, c: ((r >> 1) + 32 * g == c) & (r < 64))
        f = f + dot(column(pair, 8, g - 1), place)
        m = m + dot(column(wide, 16, g - 1), place)
    f, m = 0.5 * f, 0.125 * m
    p0 = select_matrix((128, 128), lambda r, c: ((r >> 1) + 96 == c) & (r < 64))
    p3 = select_matrix((128, 128), lambda r, c: ((r >> 1) == c) & (r < 64))
    beside = 0.125 * (dot(column(wide, 16, -2), p0) + dot(column(wide, 16, 3), p3))
    lanes = iota((16, 128), 1)
    nr, nc = lv.nrows // 2, lv.ncols // 2
    row = wrap(iota((16, 128), 0) - 4 + lax.axis_index("px") * 4, nr)
    col = wrap((lanes >> 5) - 1 + lax.axis_index("py") * 2, nc)
    prev = jnp.where(lanes < 32, pltpu.roll(beside, 32, 1), pltpu.roll(m, 32, 1))
    nxt = jnp.where(lanes >= 96, pltpu.roll(beside, 96, 1), pltpu.roll(m, 96, 1))
    d = 6.0 * m + jnp.where(row == 0, m, up(m)) + jnp.where(row == nr - 1, m, down(m))
    d = d + jnp.where(col == 0, m, prev) + jnp.where(col == nc - 1, m, nxt)
    plane = lanes & 31
    d = d + jnp.where(plane == 0, m, left(m)) + jnp.where(plane == 31, m, right(m))
    packed[0] = f
    packed[1] = m[2:10]
    packed[2] = (0.8 / d)[2:10]


def coarse_solve(groups, nr, nc, out):
    shape = (W, 128)
    lane = iota(shape, 1)
    row_ok = wrap(iota(shape, 0) - 10 + lax.axis_index("px") * 4, nr) > 0
    plane_ok = (lane & 31) > 0
    low, high = lane < 32, lane >= 96
    n = len(groups)
    f = [g[0] for g in groups]
    m = [g[1] for g in groups]
    c = [g[2] for g in groups]
    col_ok = [wrap((lane >> 5) - 9 + 4 * k + lax.axis_index("py") * 2, nc) > 0 for k in range(n)]
    zero = jnp.zeros(shape, F32)

    def before(x, k):
        a = pltpu.roll(x[k], 32, 1)
        b = pltpu.roll(x[k - 1], 32, 1) if k else zero
        return jnp.where(low, b, a)

    def after(x, k):
        a = pltpu.roll(x[k], 96, 1)
        b = pltpu.roll(x[k + 1], 96, 1) if k + 1 < n else zero
        return jnp.where(high, b, a)

    sx = [jnp.where(row_ok, a + up(a), 0.0) for a in m]
    sy = [jnp.where(col_ok[k], a + before(m, k), 0.0) for k, a in enumerate(m)]
    sz = [jnp.where(plane_ok, a + left(a), 0.0) for a in m]
    v = [a * b for a, b in zip(c, f)]
    for _ in range(7):
        wy = [a * b for a, b in zip(sy, v)]
        new = []
        for k in range(n):
            x = v[k]
            total = f[k] + sx[k] * up(x) + down(sx[k] * x)
            total = total + sy[k] * before(v, k) + after(wy, k)
            total = total + sz[k] * left(x) + right(sz[k] * x)
            new.append(0.2 * x + c[k] * total)
        v = new
    for k in range(n):
        out[k] = v[k]


def ascent_kernel(levels, own, near0, near1, far0, far1, *refs):
    fields = [refs[6 * k : 6 * k + 6] for k in range(3)]
    result = refs[18]
    e3, p2, a2, b2, p1, q1, a1, b1, p0, q0, a0 = refs[19:]
    lv0, lv1, lv2 = levels
    position, count = lax.axis_index("py"), lax.axis_size("py")

    def outer(pair, step):
        prev, nxt = chooser("py", step)(pair[0][...], pair[1][...])
        turn = lambda t: pltpu.roll(t, 64, 2)
        prev = jnp.where(position < step, turn(prev), prev)
        return prev, jnp.where(position >= count - step, turn(nxt), nxt)

    before, after = outer((near0, near1), 2)
    first, last = outer((far0, far1), 4)
    coarse_solve([first, before, own[...], after, last], lv2.nrows // 2, lv2.ncols // 2, e3)

    p2[...] = jnp.zeros(p2.shape, F32)
    two = p2.reshape(8 * W, 128)
    for q in range(-2, 4):
        group, g = (q + 9) // 4, (q + 9) % 4
        spread = select_matrix((128, 128), lambda r, c: ((c >> 1) + 32 * g == r) & (c < 64))
        x = dot(e3[group, 8:16], spread)
        two[pl.ds((2 * q) % W, 8, stride=W)] = x
        two[pl.ds((2 * q + 1) % W, 8, stride=W)] = x
    v, rhs, sx, sy, sz, coef = fields[2]

    value2 = lambda i: v[i] + p2[i // 2 - 2]
    sweep(5, 19, value2, writer(b2), rhs, sx, sy, sz, coef)
    sweep(6, 18, reader(b2), writer(a2), rhs, sx, sy, sz, coef)

    for k in range(12):
        x = a2[k + 6]
        for s in range(2):
            p1[k, pl.ds(s, 8, stride=2)] = x[0:8]
            p1[k, pl.ds(16 + s, 4, stride=2)] = x[20:24]
    q1[...] = dot(p1[...].reshape(12 * W, 128), spread_planes(128, 0, 64)).reshape(12, W, 128)
    v1, rhs1, sx1, sy1, sz1, coef1 = fields[1]

    value1 = lambda i: v1[i] + q1[i // 2 - 1]
    sweep(4, 24, value1, writer(b1), rhs1, sx1, sy1, sz1, coef1)
    sweep(5, 23, reader(b1), writer(a1), rhs1, sx1, sy1, sz1, coef1)

    for k in range(18):
        x = a1[k + 5]
        for s in range(2):
            p0[k, pl.ds(s, 8, stride=2)] = x[0:8]
            p0[k, pl.ds(16 + s, 2, stride=2)] = x[8:10]
            p0[k, pl.ds(20 + s, 2, stride=2)] = x[22:24]
    q0[...] = dot(p0[...].reshape(18 * W, 128), spread_planes(256)).reshape(18, W, 256)
    v0, rhs0, sx0, sy0, sz0, coef0 = fields[0]

    value0 = lambda i: v0[i] + q0[i // 2 - 1]
    sweep(3, 37, value0, writer(a0), rhs0, sx0, sy0, sz0, coef0)

    def final(i, x):
        result[i - 4] = x[0:16]

    sweep(4, 36, reader(a0), final, rhs0, sx0, sy0, sz0, coef0)


VMEM = pl.BlockSpec(memory_space=pltpu.VMEM)
LIMIT = 14 << 20


def descend(kernel, lv, inputs, packed, scratch):
    block = jax.ShapeDtypeStruct((lv.total, W, lv.lanes), F32)
    outs = pl.pallas_call(
        lambda *refs: kernel(lv, *refs),
        out_shape=[jax.ShapeDtypeStruct(packed, F32)] + [block] * 6,
        in_specs=[VMEM] * len(inputs),
        out_specs=[VMEM] * 7,
        scratch_shapes=[pltpu.VMEM(block.shape, F32)] * 3 + [pltpu.VMEM(s, F32) for s in scratch],
        compiler_params=pltpu.CompilerParams(vmem_limit_bytes=LIMIT),
        name="descent",
    )(*inputs)
    return outs[0], outs[1:]


def is_odd(axis, step):
    return (lax.axis_index(axis) & step) != 0


def swap_partners(n, step, parity):
    partner = list(range(n))
    for i in range(n - step):
        if (i // step) % 2 == parity:
            partner[i], partner[i + step] = i + step, i
    alone = [i for i in range(n) if partner[i] == i]
    for group in (alone[:step], alone[step:]):
        for i, j in zip(group, reversed(group)):
            partner[i] = j
    return partner


def exchange(to_prev, to_next, odd, axis, step=1):
    n, other = lax.axis_size(axis), "py" if axis == "px" else "px"
    got = []
    for parity in range(2):
        partner = swap_partners(n, step, parity)
        pairs = []
        for i in range(n):
            for j in range(lax.axis_size(other)):
                a, b = (i, j), (partner[i], j if partner[i] != i else j ^ 1)
                if axis == "py":
                    a, b = a[::-1], b[::-1]
                pairs.append(tuple(p * lax.axis_size("py") + q for p, q in (a, b)))
        if to_prev is None:
            out = to_next[parity]
        elif to_prev is to_next:
            out = to_next
        else:
            out = jnp.where(odd == (parity == 0), to_prev, to_next)
        got.append(lax.ppermute(out, ("px", "py"), pairs))
    return got


def pick(got, odd):
    return jnp.where(odd, got[0], got[1]), jnp.where(odd, got[1], got[0])


def per_device(source, density):
    npx, npy = lax.axis_size("px"), lax.axis_size("py")
    lv0 = Level(32, 4, 16, 4, 256, 256, 32 * npx, 16 * npy)
    lv1 = Level(16, 6, 8, 8, 128, 128, 16 * npx, 8 * npy)
    lv2 = Level(8, 8, 4, 8, 128, 64, 8 * npx, 4 * npy)

    x, step_rows = lax.axis_index("px"), 2
    flags = (
        is_odd("px", 1), is_odd("py", 1), is_odd("px", step_rows),
        x < step_rows, x >= npx - step_rows,
        ((1 - (x & 1)) * (lv0.rows - lv0.halo), (x & 1) * (lv0.rows - lv0.halo)),
    )
    source, density, (odd_x, odd_y, odd_2, first_x, last_x, starts) = lax.optimization_barrier(
        (source, density, flags)
    )

    h = lv0.halo
    edge_rows = [
        jnp.concatenate([lax.dynamic_slice_in_dim(a, at, h, 0) for a in (source, density)], 0)
        for at in starts
    ]
    rows = exchange(None, edge_rows, odd_x, "px")
    lo, hi = pick(rows, odd_x)
    to_right = lambda s, d: jnp.concatenate([d[:, 12:16], s[:, 12:16]], 1)
    to_left = lambda s, d: jnp.concatenate([s[:, 0:4], d[:, 0:4]], 1)
    sides = exchange(to_left(source, density), to_right(source, density), odd_y, "py")
    row_source = jnp.concatenate([lo[:h], hi[:h]], 0)
    row_density = jnp.concatenate([lo[h:], hi[h:]], 0)
    corners = exchange(
        to_left(row_source, row_density), to_right(row_source, row_density), odd_y, "py"
    )
    one, saved0 = descend(
        level0_kernel, lv0, (source, density, *rows, *sides, *corners),
        (16, W, 128), [(16, W, 256), (16 * W, 128)],
    )

    h = lv1.halo
    rows = exchange(one[:h], one[-h:], odd_x, "px")
    lo, hi = pick(rows, odd_x)
    wide = lambda a: jnp.concatenate([lo[:, a : a + 8], one[:, a : a + 8], hi[:, a : a + 8]], 0)
    sides = exchange(wide(8), wide(0), odd_y, "py")
    two, saved1 = descend(
        level1_kernel, lv1, (one, *rows, *sides), (8, 16, 128), [(8, W, 128), (8 * W, 128)],
    )

    rows = exchange(two, two, odd_x, "px")
    lo, hi = pick(rows, odd_x)
    wide = lambda a: jnp.concatenate([lo[:, a : a + 8], two[:, a : a + 8], hi[:, a : a + 8]], 0)
    sides = exchange(wide(8), wide(0), odd_y, "py")
    three, saved2 = descend(
        level2_kernel, lv2, (two, *rows, *sides), (3, 8, 128), [(8, W, 128), (16, W, 128)],
    )

    lo, hi = pick(exchange(three, three, odd_2, "px", step_rows), odd_2)
    turn = lambda t: jnp.concatenate([t[:, 4:], t[:, :4]], 1)
    lo, hi = jnp.where(first_x, turn(lo), lo), jnp.where(last_x, turn(hi), hi)
    wide = jnp.concatenate([lo, three, hi], 1)
    groups = (wide, *exchange(wide, wide, None, "py", 2), *exchange(wide, wide, None, "py", 4))
    inputs = (*groups, *saved0, *saved1, *saved2)
    shapes = [(5, W, 128), (8, W, 128), (24, W, 128), (24, W, 128), (12, W, 128), (12, W, 128),
              (28, W, 128), (28, W, 128), (18, W, 128), (18, W, 256), (40, W, 256)]
    return pl.pallas_call(
        lambda *refs: ascent_kernel((lv0, lv1, lv2), *refs),
        out_shape=jax.ShapeDtypeStruct(source.shape, F32),
        in_specs=[VMEM] * len(inputs),
        out_specs=VMEM,
        scratch_shapes=[pltpu.VMEM(s, F32) for s in shapes],
        compiler_params=pltpu.CompilerParams(vmem_limit_bytes=LIMIT),
        name="ascent",
    )(*inputs)


def solution(mesh):
    spec = P("px", "py", None)
    return jax.shard_map(
        per_device, mesh=mesh, in_specs=(spec, spec), out_specs=spec, check_vma=False
    )
```

```python
import jax
import jax.numpy as jnp
from jax import lax
from jax.experimental import pallas as pl
from jax.experimental.pallas import tpu as pltpu
from jax.sharding import PartitionSpec as P

F32 = jnp.float32
W = 24
BF16 = jnp.bfloat16
UNROLL = 4


def iota(shape, dim):
    return lax.broadcasted_iota(jnp.int32, shape, dim)


def up(x):
    return pltpu.roll(x, 1, 0)


def down(x):
    return pltpu.roll(x, x.shape[0] - 1, 0)


def left(x):
    return pltpu.roll(x, 1, 1)


def right(x):
    return pltpu.roll(x, x.shape[1] - 1, 1)


def dot(a, b):
    high = a.astype(BF16)
    rest = a - high.astype(F32)
    mid = rest.astype(BF16)
    low = (rest - mid.astype(F32)).astype(BF16)
    return sum(jnp.dot(x, b, preferred_element_type=F32) for x in (high, mid, low))


def select_matrix(shape, where):
    return jnp.where(where(iota(shape, 0), iota(shape, 1)), 1.0, 0.0).astype(BF16)


def wrap(x, n):
    return jnp.where(x < 0, x + n, jnp.where(x >= n, x - n, x))


class Level:
    def __init__(self, rows, halo, cols, right_cols, lanes, planes, nrows, ncols):
        self.rows, self.halo, self.cols, self.right_cols = rows, halo, cols, right_cols
        self.lanes, self.planes, self.nrows, self.ncols = lanes, planes, nrows, ncols
        self.total = rows + 2 * halo

    def masks(self):
        shape = (W, self.lanes)
        col = iota(shape, 0)
        col = jnp.where(col < self.cols + self.right_cols, col, col - W)
        col = wrap(col + lax.axis_index("py") * self.cols, self.ncols)
        lane = iota(shape, 1)
        edge = lambda hit: jnp.where(hit, 2.0, 0.0)
        extra = edge(col == 0) + edge(col == self.ncols - 1)
        extra = extra + edge(lane == 0) + edge(lane == self.planes - 1)
        return lane < self.planes, col > 0, (lane > 0) & (lane < self.planes), extra

    def global_row(self, i):
        return wrap(lax.axis_index("px") * self.rows - self.halo + i, self.nrows)


def prepare(level, mob, rhs, sx, sy, sz, coef, diag, out):
    inside, inner_col, inner_plane, extra = level.masks()

    def face(i, a, b):
        return (a + b) * jnp.where(level.global_row(i) == 0, 0.0, 1.0)

    def step(i, carry):
        m, wx = carry
        below = mob[i + 1]
        g = level.global_row(i)
        next_wx = face(i + 1, m, below)
        wy = jnp.where(inner_col, m + up(m), 0.0)
        wz = jnp.where(inner_plane, m + left(m), 0.0)
        sx[i + 1] = next_wx
        sy[i] = wy
        sz[i] = wz
        ends = jnp.where((g == 0) | (g == level.nrows - 1), 2.0, 0.0)
        d = (wx + next_wx) + (wy + down(wy)) + (wz + right(wz)) + (extra + ends) * m
        c = 0.8 / d
        if level.planes < level.lanes:
            c = jnp.where(inside, c, 0.0)
        coef[i] = c
        diag[i] = d
        out[i] = c * rhs[i]
        return below, next_wx

    first = face(1, mob[0], mob[1])
    sx[1] = first
    lax.fori_loop(1, level.total - 1, step, (mob[1], first), unroll=level.total - 2)


def walk(lo, hi, load, emit, sx, sy, sz):
    def step(i, carry):
        above, c, wx = carry
        below, next_wx = load(i + 1), sx[i + 1]
        wy, wz = sy[i], sz[i]
        total = (wx * above + next_wx * below) + (wy * up(c) + down(wy * c))
        total = total + (wz * left(c) + right(wz * c))
        emit(i, c, total)
        return c, below, next_wx

    unroll = hi - lo
    lax.fori_loop(lo, hi, step, (load(lo - 1), load(lo), sx[lo]), unroll=unroll)


def sweep(lo, hi, load, store, rhs, sx, sy, sz, coef):
    def emit(i, c, total):
        store(i, 0.2 * c + coef[i] * (rhs[i] + total))

    walk(lo, hi, load, emit, sx, sy, sz)


def reader(ref):
    return lambda i: ref[i]


def writer(ref):
    def store(i, x):
        ref[i] = x

    return store


def paired_residual(pairs, lo, cols, v, out, rhs, sx, sy, sz, diag):
    def step(k, carry):
        above, c, wx = carry
        done = []
        for j in range(2):
            i = lo + 2 * k + j
            below, next_wx = v[i + 1], sx[i + 1]
            wy, wz = sy[i], sz[i]
            total = (wx * above + next_wx * below) + (wy * up(c) + down(wy * c))
            total = total + (wz * left(c) + right(wz * c))
            done.append((rhs[i] - diag[i] * c + total)[0:cols])
            above, c, wx = c, below, next_wx
        out[k] = done[0] + done[1]
        return above, c, wx

    lax.fori_loop(0, pairs, step, (v[lo - 1], v[lo], sx[lo]), unroll=pairs)


def pair_planes(lanes_in, offset=0, lanes_out=128):
    return select_matrix((lanes_in, lanes_out), lambda r, c: (r >> 1) + offset == c)


def spread_planes(lanes_out, offset=0, planes=128):
    return select_matrix((128, lanes_out), lambda r, c: ((c >> 1) + offset == r) & ((c >> 1) < planes))


def chooser(axis, step=1):
    odd = is_odd(axis, step)
    return lambda a, b: (jnp.where(odd, a, b), jnp.where(odd, b, a))


def halo_readers(rows0, rows1):
    choose = chooser("px")
    lo = lambda i: choose(rows0[i], rows1[i])[0]
    hi = lambda i: choose(rows0[i], rows1[i])[1]
    return lo, hi, chooser("py")


def level0_kernel(lv, src, dens, rows0, rows1, sides0, sides1, corners0, corners1, packed, v, rhs, sx, sy, sz, coef,
                  mob, first, diag, pair, low):
    h = lv.halo
    tile = iota((8, lv.lanes), 0)
    lo, hi, choose = halo_readers(rows0, rows1)

    def load(i, s, d, a, b):
        rhs[i, 0:16] = 2.0 * s
        mob[i, 0:16] = 1.0 / d
        rhs[i, 16:24] = 2.0 * jnp.where(tile < 4, a, b)
        mob[i, 16:24] = 1.0 / pltpu.roll(jnp.where(tile < 4, b, a), 4, 0)

    for i in range(h):
        left_side, right_side = choose(corners0[i], corners1[i])
        load(i, lo(i), lo(h + i), right_side, left_side)
        left_side, right_side = choose(corners0[h + i], corners1[h + i])
        load(lv.total - h + i, hi(i), hi(h + i), right_side, left_side)

    def body(i, carry):
        left_side, right_side = choose(sides0[i], sides1[i])
        load(h + i, src[i], dens[i], right_side, left_side)
        return carry

    lax.fori_loop(0, lv.rows, body, 0, unroll=lv.rows)
    zero = jnp.zeros((W, lv.lanes), F32)
    for ref in (first, v):
        ref[0] = zero
        ref[lv.total - 1] = zero
    prepare(lv, mob, rhs, sx, sy, sz, coef, diag, first)
    sweep(1, lv.total - 1, reader(first), writer(v), rhs, sx, sy, sz, coef)
    half = lv.rows // 2
    z = pair_planes(lv.lanes)
    paired_residual(half, h, 16, v, pair.at[:, 0:16], rhs, sx, sy, sz, diag)

    low[0 : half * 16] = 0.5 * dot(pair[:, 0:16].reshape(half * 16, lv.lanes), z)
    fine = low[pl.ds(0, half * 8, stride=2)] + low[pl.ds(1, half * 8, stride=2)]

    def mobs(k, carry):
        pair[k] = mob[h + 2 * k] + mob[h + 2 * k + 1]
        return carry

    lax.fori_loop(0, half, mobs, 0, unroll=half)
    low[...] = 0.125 * dot(pair[...].reshape(half * W, lv.lanes), z)
    at = iota((8, 128), 0)
    beside = jnp.zeros((4, 128), F32)
    for k in range(half):
        f = fine[8 * k : 8 * k + 8]
        m = low[pl.ds(k * W, 8, stride=2)] + low[pl.ds(k * W + 1, 8, stride=2)]
        e = low[pl.ds(k * W + 16, 4, stride=2)] + low[pl.ds(k * W + 17, 4, stride=2)]
        e = pltpu.roll(jnp.concatenate([e, beside], 0), 2, 0)
        shifted = pltpu.roll(m, 2, 0)
        packed[k, 0:8] = jnp.where(at < 4, pltpu.roll(f, 4, 0), shifted)
        packed[k, 8:16] = jnp.where(at < 4, f, shifted)
        packed[k, 16:24] = jnp.where((at < 2) | (at >= 6), m, e)


def level1_kernel(lv, own, rows0, rows1, sides0, sides1, packed, v, rhs, sx, sy, sz, coef,
                  mob, first, diag, pair, low):
    h = lv.halo

    at = iota((8, lv.lanes), 0)
    lo, hi, choose = halo_readers(rows0, rows1)

    def load(i, block):
        t0, t1, t2 = block[0:8], block[8:16], block[16:24]
        b, a = choose(sides0[i], sides1[i])
        rhs[i, 0:8] = jnp.where(at < 4, t1, pltpu.roll(t0, 4, 0))
        rhs[i, 8:16] = a
        rhs[i, 16:24] = pltpu.roll(b, 4, 0)
        mob[i, 0:8] = jnp.where((at < 2) | (at >= 6), t2, pltpu.roll(t0, 6, 0))
        far = jnp.where(at < 6, pltpu.roll(a, 6, 0), 1.0)
        mob[i, 8:16] = jnp.where(at < 2, pltpu.roll(t2, 6, 0), far)
        far = jnp.where(at < 2, 1.0, pltpu.roll(b, 6, 0))
        mob[i, 16:24] = jnp.where(at < 6, far, pltpu.roll(t2, 2, 0))

    for i in range(h):
        load(i, lo(i))
        load(lv.total - h + i, hi(i))

    def body(i, carry):
        load(h + i, own[i])
        return carry

    lax.fori_loop(0, lv.rows, body, 0, unroll=lv.rows)
    zero = jnp.zeros((W, lv.lanes), F32)
    for ref in (first, v):
        ref[0] = zero
        ref[lv.total - 1] = zero
    prepare(lv, mob, rhs, sx, sy, sz, coef, diag, first)
    sweep(1, lv.total - 1, reader(first), writer(v), rhs, sx, sy, sz, coef)
    half = lv.rows // 2
    paired_residual(half, h, W, v, pair, rhs, sx, sy, sz, diag)
    x = 0.5 * dot(pair[...].reshape(half * W, lv.lanes), pair_planes(lv.lanes))

    def mobs(k, carry):
        pair[k] = mob[h + 2 * k] + mob[h + 2 * k + 1]
        return carry

    lax.fori_loop(0, half, mobs, 0, unroll=half)
    low[...] = x + 0.125 * dot(pair[...].reshape(half * W, lv.lanes), pair_planes(lv.lanes, 64))
    for k in range(half):
        a = k * W
        y = low[pl.ds(a, 8, stride=2)] + low[pl.ds(a + 1, 8, stride=2)]
        packed[k, 8:16] = y
        packed[k, 4:8] = y[0:4]
        packed[k, 0:4] = low[pl.ds(a + 16, 4, stride=2)] + low[pl.ds(a + 17, 4, stride=2)]


def level2_kernel(lv, own, rows0, rows1, sides0, sides1, packed, v, rhs, sx, sy, sz, coef,
                  mob, first, diag, pair, wide):
    h = lv.halo
    tile = iota((8, 128), 0)
    lane = iota((8, 128), 1) < lv.planes
    lo, hi, choose = halo_readers(rows0, rows1)

    def load(i, block):
        l, r = choose(sides0[i], sides1[i])
        r = pltpu.roll(r, 4, 0)
        parts = (jnp.where(tile < 4, block, r), r, l)
        for k, part in enumerate(parts):
            rhs[i, 8 * k : 8 * k + 8] = jnp.where(lane, part, 0.0)
            mob[i, 8 * k : 8 * k + 8] = jnp.where(lane, pltpu.roll(part, 64, 1), 1.0)

    for i in range(h):
        load(i, lo(i)[8:16])
        load(h + i, own[i, 8:16])
        load(2 * h + i, hi(i)[8:16])
    zero = jnp.zeros((W, lv.lanes), F32)
    for ref in (first, v):
        ref[0] = zero
        ref[lv.total - 1] = zero
    prepare(lv, mob, rhs, sx, sy, sz, coef, diag, first)
    sweep(1, lv.total - 1, reader(first), writer(v), rhs, sx, sy, sz, coef)
    paired_residual(8, 4, W, v, pair, rhs, sx, sy, sz, diag)
    for k in range(12):
        wide[k] = mob[2 * k] + mob[2 * k + 1]
    for k in range(12, 16):
        wide[k] = zero

    def column(ref, n, q):
        two = ref.reshape(n * W, 128)
        return two[pl.ds((2 * q) % W, n, stride=W)] + two[pl.ds((2 * q + 1) % W, n, stride=W)]

    f = jnp.zeros((8, 128), F32)
    m = jnp.zeros((16, 128), F32)
    for g in range(4):
        place = select_matrix((128, 128), lambda r, c: ((r >> 1) + 32 * g == c) & (r < 64))
        f = f + dot(column(pair, 8, g - 1), place)
        m = m + dot(column(wide, 16, g - 1), place)
    f, m = 0.5 * f, 0.125 * m
    p0 = select_matrix((128, 128), lambda r, c: ((r >> 1) + 96 == c) & (r < 64))
    p3 = select_matrix((128, 128), lambda r, c: ((r >> 1) == c) & (r < 64))
    beside = 0.125 * (dot(column(wide, 16, -2), p0) + dot(column(wide, 16, 3), p3))
    lanes = iota((16, 128), 1)
    nr, nc = lv.nrows // 2, lv.ncols // 2
    row = wrap(iota((16, 128), 0) - 4 + lax.axis_index("px") * 4, nr)
    col = wrap((lanes >> 5) - 1 + lax.axis_index("py") * 2, nc)
    prev = jnp.where(lanes < 32, pltpu.roll(beside, 32, 1), pltpu.roll(m, 32, 1))
    nxt = jnp.where(lanes >= 96, pltpu.roll(beside, 96, 1), pltpu.roll(m, 96, 1))
    d = 6.0 * m + jnp.where(row == 0, m, up(m)) + jnp.where(row == nr - 1, m, down(m))
    d = d + jnp.where(col == 0, m, prev) + jnp.where(col == nc - 1, m, nxt)
    plane = lanes & 31
    d = d + jnp.where(plane == 0, m, left(m)) + jnp.where(plane == 31, m, right(m))
    packed[0] = f
    packed[1] = m[2:10]
    packed[2] = (0.8 / d)[2:10]


def coarse_solve(groups, nr, nc, out):
    shape = (W, 128)
    lane = iota(shape, 1)
    row_ok = wrap(iota(shape, 0) - 10 + lax.axis_index("px") * 4, nr) > 0
    plane_ok = (lane & 31) > 0
    low, high = lane < 32, lane >= 96
    n = len(groups)
    f = [g[0] for g in groups]
    m = [g[1] for g in groups]
    c = [g[2] for g in groups]
    col_ok = [wrap((lane >> 5) - 9 + 4 * k + lax.axis_index("py") * 2, nc) > 0 for k in range(n)]
    zero = jnp.zeros(shape, F32)

    def before(x, k):
        a = pltpu.roll(x[k], 32, 1)
        b = pltpu.roll(x[k - 1], 32, 1) if k else zero
        return jnp.where(low, b, a)

    def after(x, k):
        a = pltpu.roll(x[k], 96, 1)
        b = pltpu.roll(x[k + 1], 96, 1) if k + 1 < n else zero
        return jnp.where(high, b, a)

    sx = [jnp.where(row_ok, a + up(a), 0.0) for a in m]
    sy = [jnp.where(col_ok[k], a + before(m, k), 0.0) for k, a in enumerate(m)]
    sz = [jnp.where(plane_ok, a + left(a), 0.0) for a in m]
    v = [a * b for a, b in zip(c, f)]
    for _ in range(7):
        wy = [a * b for a, b in zip(sy, v)]
        new = []
        for k in range(n):
            x = v[k]
            total = f[k] + sx[k] * up(x) + down(sx[k] * x)
            total = total + sy[k] * before(v, k) + after(wy, k)
            total = total + sz[k] * left(x) + right(sz[k] * x)
            new.append(0.2 * x + c[k] * total)
        v = new
    for k in range(n):
        out[k] = v[k]


def ascent_kernel(levels, own, near0, near1, far0, far1, *refs):
    fields = [refs[6 * k : 6 * k + 6] for k in range(3)]
    result = refs[18]
    e3, p2, a2, b2, p1, q1, a1, b1, p0, q0, a0 = refs[19:]
    lv0, lv1, lv2 = levels
    position, count = lax.axis_index("py"), lax.axis_size("py")

    def outer(pair, step):
        prev, nxt = chooser("py", step)(pair[0][...], pair[1][...])
        turn = lambda t: pltpu.roll(t, 64, 2)
        prev = jnp.where(position < step, turn(prev), prev)
        return prev, jnp.where(position >= count - step, turn(nxt), nxt)

    before, after = outer((near0, near1), 2)
    first, last = outer((far0, far1), 4)
    coarse_solve([first, before, own[...], after, last], lv2.nrows // 2, lv2.ncols // 2, e3)

    p2[...] = jnp.zeros(p2.shape, F32)
    two = p2.reshape(8 * W, 128)
    for q in range(-2, 4):
        group, g = (q + 9) // 4, (q + 9) % 4
        spread = select_matrix((128, 128), lambda r, c: ((c >> 1) + 32 * g == r) & (c < 64))
        x = dot(e3[group, 8:16], spread)
        two[pl.ds((2 * q) % W, 8, stride=W)] = x
        two[pl.ds((2 * q + 1) % W, 8, stride=W)] = x
    v, rhs, sx, sy, sz, coef = fields[2]

    value2 = lambda i: v[i] + p2[i // 2 - 2]
    sweep(5, 19, value2, writer(b2), rhs, sx, sy, sz, coef)
    sweep(6, 18, reader(b2), writer(a2), rhs, sx, sy, sz, coef)

    for k in range(12):
        x = a2[k + 6]
        for s in range(2):
            p1[k, pl.ds(s, 8, stride=2)] = x[0:8]
            p1[k, pl.ds(16 + s, 4, stride=2)] = x[20:24]
    q1[...] = dot(p1[...].reshape(12 * W, 128), spread_planes(128, 0, 64)).reshape(12, W, 128)
    v1, rhs1, sx1, sy1, sz1, coef1 = fields[1]

    value1 = lambda i: v1[i] + q1[i // 2 - 1]
    sweep(4, 24, value1, writer(b1), rhs1, sx1, sy1, sz1, coef1)
    sweep(5, 23, reader(b1), writer(a1), rhs1, sx1, sy1, sz1, coef1)

    for k in range(18):
        x = a1[k + 5]
        for s in range(2):
            p0[k, pl.ds(s, 8, stride=2)] = x[0:8]
            p0[k, pl.ds(16 + s, 2, stride=2)] = x[8:10]
            p0[k, pl.ds(20 + s, 2, stride=2)] = x[22:24]
    q0[...] = dot(p0[...].reshape(18 * W, 128), spread_planes(256)).reshape(18, W, 256)
    v0, rhs0, sx0, sy0, sz0, coef0 = fields[0]

    value0 = lambda i: v0[i] + q0[i // 2 - 1]
    sweep(3, 37, value0, writer(a0), rhs0, sx0, sy0, sz0, coef0)

    def final(i, x):
        result[i - 4] = x[0:16]

    sweep(4, 36, reader(a0), final, rhs0, sx0, sy0, sz0, coef0)


VMEM = pl.BlockSpec(memory_space=pltpu.VMEM)
LIMIT = 14 << 20


def descend(kernel, lv, inputs, packed, scratch):
    block = jax.ShapeDtypeStruct((lv.total, W, lv.lanes), F32)
    outs = pl.pallas_call(
        lambda *refs: kernel(lv, *refs),
        out_shape=[jax.ShapeDtypeStruct(packed, F32)] + [block] * 6,
        in_specs=[VMEM] * len(inputs),
        out_specs=[VMEM] * 7,
        scratch_shapes=[pltpu.VMEM(block.shape, F32)] * 3 + [pltpu.VMEM(s, F32) for s in scratch],
        compiler_params=pltpu.CompilerParams(vmem_limit_bytes=LIMIT),
        name="descent",
    )(*inputs)
    return outs[0], outs[1:]


def is_odd(axis, step):
    return (lax.axis_index(axis) & step) != 0


def swap_partners(n, step, parity):
    partner = list(range(n))
    for i in range(n - step):
        if (i // step) % 2 == parity:
            partner[i], partner[i + step] = i + step, i
    alone = [i for i in range(n) if partner[i] == i]
    for group in (alone[:step], alone[step:]):
        for i, j in zip(group, reversed(group)):
            partner[i] = j
    return partner


def exchange(to_prev, to_next, odd, axis, step=1):
    n, other = lax.axis_size(axis), "py" if axis == "px" else "px"
    got = []
    for parity in range(2):
        partner = swap_partners(n, step, parity)
        pairs = []
        for i in range(n):
            for j in range(lax.axis_size(other)):
                a, b = (i, j), (partner[i], j if partner[i] != i else j ^ 1)
                if axis == "py":
                    a, b = a[::-1], b[::-1]
                pairs.append(tuple(p * lax.axis_size("py") + q for p, q in (a, b)))
        if to_prev is None:
            out = to_next[parity]
        elif to_prev is to_next:
            out = to_next
        else:
            out = jnp.where(odd == (parity == 0), to_prev, to_next)
        got.append(lax.ppermute(out, ("px", "py"), pairs))
    return got


def pick(got, odd):
    return jnp.where(odd, got[0], got[1]), jnp.where(odd, got[1], got[0])


def per_device(source, density):
    npx, npy = lax.axis_size("px"), lax.axis_size("py")
    lv0 = Level(32, 4, 16, 4, 256, 256, 32 * npx, 16 * npy)
    lv1 = Level(16, 6, 8, 8, 128, 128, 16 * npx, 8 * npy)
    lv2 = Level(8, 8, 4, 8, 128, 64, 8 * npx, 4 * npy)

    x, step_rows = lax.axis_index("px"), 2
    flags = (
        is_odd("px", 1), is_odd("py", 1), is_odd("px", step_rows),
        x < step_rows, x >= npx - step_rows,
        ((1 - (x & 1)) * (lv0.rows - lv0.halo), (x & 1) * (lv0.rows - lv0.halo)),
    )
    source, density, (odd_x, odd_y, odd_2, first_x, last_x, starts) = lax.optimization_barrier(
        (source, density, flags)
    )

    h = lv0.halo
    edge_rows = [
        jnp.concatenate([lax.dynamic_slice_in_dim(a, at, h, 0) for a in (source, density)], 0)
        for at in starts
    ]
    rows = exchange(None, edge_rows, odd_x, "px")
    lo, hi = pick(rows, odd_x)
    to_right = lambda s, d: jnp.concatenate([d[:, 12:16], s[:, 12:16]], 1)
    to_left = lambda s, d: jnp.concatenate([s[:, 0:4], d[:, 0:4]], 1)
    sides = exchange(to_left(source, density), to_right(source, density), odd_y, "py")
    row_source = jnp.concatenate([lo[:h], hi[:h]], 0)
    row_density = jnp.concatenate([lo[h:], hi[h:]], 0)
    corners = exchange(
        to_left(row_source, row_density), to_right(row_source, row_density), odd_y, "py"
    )
    one, saved0 = descend(
        level0_kernel, lv0, (source, density, *rows, *sides, *corners),
        (16, W, 128), [(16, W, 256), (16 * W, 128)],
    )

    h = lv1.halo
    rows = exchange(one[:h], one[-h:], odd_x, "px")
    lo, hi = pick(rows, odd_x)
    wide = lambda a: jnp.concatenate([lo[:, a : a + 8], one[:, a : a + 8], hi[:, a : a + 8]], 0)
    sides = exchange(wide(8), wide(0), odd_y, "py")
    two, saved1 = descend(
        level1_kernel, lv1, (one, *rows, *sides), (8, 16, 128), [(8, W, 128), (8 * W, 128)],
    )

    rows = exchange(two, two, odd_x, "px")
    lo, hi = pick(rows, odd_x)
    wide = lambda a: jnp.concatenate([lo[:, a : a + 8], two[:, a : a + 8], hi[:, a : a + 8]], 0)
    sides = exchange(wide(8), wide(0), odd_y, "py")
    three, saved2 = descend(
        level2_kernel, lv2, (two, *rows, *sides), (3, 8, 128), [(8, W, 128), (16, W, 128)],
    )

    lo, hi = pick(exchange(three, three, odd_2, "px", step_rows), odd_2)
    turn = lambda t: jnp.concatenate([t[:, 4:], t[:, :4]], 1)
    lo, hi = jnp.where(first_x, turn(lo), lo), jnp.where(last_x, turn(hi), hi)
    wide = jnp.concatenate([lo, three, hi], 1)
    groups = (wide, *exchange(wide, wide, None, "py", 2), *exchange(wide, wide, None, "py", 4))
    inputs = (*groups, *saved0, *saved1, *saved2)
    shapes = [(5, W, 128), (8, W, 128), (24, W, 128), (24, W, 128), (12, W, 128), (12, W, 128),
              (28, W, 128), (28, W, 128), (18, W, 128), (18, W, 256), (40, W, 256)]
    return pl.pallas_call(
        lambda *refs: ascent_kernel((lv0, lv1, lv2), *refs),
        out_shape=jax.ShapeDtypeStruct(source.shape, F32),
        in_specs=[VMEM] * len(inputs),
        out_specs=VMEM,
        scratch_shapes=[pltpu.VMEM(s, F32) for s in shapes],
        compiler_params=pltpu.CompilerParams(vmem_limit_bytes=LIMIT),
        name="ascent",
    )(*inputs)


def solution(mesh):
    spec = P("px", "py", None)
    return jax.shard_map(
        per_device, mesh=mesh, in_specs=(spec, spec), out_specs=spec, check_vma=False
    )
```
